128 devices in a mesh: rows: 32 (over z, y, core), fib: 4 (over x).
Axes of the slice: x: 4, y: 4, z: 4, core: 2. Of those that a mesh axis runs over, the one named last changes fastest.
Arguments:
- frames: bfloat16 [20, 4096, 4096], P('fib', 'rows'), may hold values from 0 to 2
- amplitude: float32 [20, 512], P('fib'), may hold values from 0.5 to 2
- line_start: int32 [20, 24], P('fib'), may hold values from 0 to 4088
- bundle_width: float32 [20], replicated, may hold values from 0.8 to 1.6
- fiber_bundle: int32 [512], replicated, may hold values from 0 to 19
- trace_coef: float32 [512, 11], P(('rows', 'fib')), may hold values from -1 to 1
- width_coef: float32 [512, 11], P(('rows', 'fib')), may hold values from -0.15 to 0.15
Outputs:
- trace_fit: float32 [512, 11], P(('rows', 'fib'))
- width_fit: float32 [512, 11], P(('rows', 'fib'))
- residual: bfloat16 [20, 4096, 4096], P('fib', 'rows')
The draws below stay inside these ranges and needn't reach their ends.
All inputs are finite; a program needn't handle non-finite values.
Results may differ from the reference program's by a relative error of at most 0.001.
Values sent between devices are 32-bit elements; how exact they have to be, the bound alone decides.
A program may use at most 128 MiB of HBM per device.

```python
import math
import jax
import jax.numpy as jnp
from jax import lax

K = 11
LAMPS = 20
PIX = 8
LINES = 24
WIN = 8
BUNDLES = 20
ITERS = 3
FIBERS = 512
COLS = 4096
NR = 4096


def place_ends(result, own_key, least, largest):
    longest = result.shape.index(max(result.shape))
    spots = []
    for shift in (0, 1):
        where = [jax.random.randint(jax.random.fold_in(own_key, axis), (), 0, length) for axis, length in enumerate(result.shape)]
        where[longest] = (where[longest] + shift) % result.shape[longest]
        spots.append(tuple(where))
    return result.at[spots[0]].set(least).at[spots[1]].set(largest)


def level_of(key, extent, cuts, least, high):
    loudness, own = 1.0, jax.random.fold_in(key, 6)
    for position, blocks in cuts:
        steps = jnp.exp(jax.random.uniform(jax.random.fold_in(own, position), (blocks,), jnp.float32, least / len(cuts), high / len(cuts)))
        loudness = loudness * jnp.repeat(steps, extent[position] // blocks).reshape([-1 if axis == position else 1 for axis in range(len(extent))])
    return loudness


def bell_draw(own_key, shape, deviation, limit, cuts=(), kind=jnp.bfloat16):
    entries = deviation * jax.random.normal(own_key, shape, jnp.float32)
    if cuts:
        entries = entries * level_of(own_key, shape, cuts, -0.22, 0.18)
    return jnp.clip(entries, -limit, limit).astype(kind)


def setup_inputs(seed: int = 0) -> dict:
    streams_of = jax.random.split(jax.random.key(seed), 8)
    return {
        "frames": jnp.clip(2.0 * jax.random.uniform(streams_of[0], (LAMPS, NR, COLS), jnp.float32) ** level_of(streams_of[0], (LAMPS, NR, COLS), ((0, 4), (1, 32)), -0.2, 0.2), 0.0, 2.0).astype(jnp.bfloat16),
        "amplitude": jnp.clip(jnp.exp(math.log(2.0) - 1.3862944 * jax.random.uniform(streams_of[1], (LAMPS, FIBERS), jnp.float32) ** level_of(streams_of[1], (LAMPS, FIBERS), ((0, 4),), -0.2, 0.2)), 0.5, 2.0),
        "line_start": place_ends(jax.random.randint(streams_of[2], (LAMPS, LINES), 0, NR - WIN + 1), jax.random.fold_in(streams_of[2], 1), 0, NR - WIN).astype(jnp.int32),
        "bundle_width": jnp.clip(jnp.exp(jax.random.uniform(streams_of[3], (BUNDLES,), jnp.float32, math.log(0.8), math.log(1.6))), 0.8, 1.6),
        "fiber_bundle": place_ends(jax.random.randint(streams_of[4], (FIBERS,), 0, BUNDLES), jax.random.fold_in(streams_of[4], 1), 0, BUNDLES - 1).astype(jnp.int32),
        "trace_coef": bell_draw(streams_of[5], (FIBERS, K), 0.3, 1.0, ((0, 128),), jnp.float32),
        "width_coef": bell_draw(streams_of[6], (FIBERS, K), 0.05, 0.15, ((0, 128),), jnp.float32),
    }


HIGH = lax.Precision.HIGHEST

def legendre_table(first, count, total):
    rowpos = (first + jnp.arange(count, dtype=jnp.int32)).astype(jnp.float32)
    tvals = (2.0 * rowpos + 1.0) / total - 1.0
    polys = [jnp.ones_like(tvals), tvals]
    for order in range(1, K - 1):
        polys.append(((2 * order + 1) * tvals * polys[order] - order * polys[order - 1]) / (order + 1))
    return jnp.stack(polys[:K], axis=1)

def lit_rows(line_start, first, count):
    rowid = first + jnp.arange(count, dtype=jnp.int32)
    low = line_start[:, None, :]
    inside = (rowid[None, :, None] >= low) & (rowid[None, :, None] < low + WIN)
    return jnp.any(inside, axis=2).astype(jnp.float32)

def profile_cols(trace, width, bundle_width, fiber_bundle, ptab):
    onehot = (fiber_bundle[:, None] == jnp.arange(bundle_width.shape[0], dtype=jnp.int32)[None, :]).astype(jnp.float32)
    base = jnp.dot(onehot, bundle_width, precision=HIGH)
    centre = jnp.dot(ptab, trace.T, precision=HIGH)
    spread = base[None, :] * jnp.exp(jnp.dot(ptab, width.T, precision=HIGH))
    offsets = jnp.arange(PIX, dtype=jnp.float32) - (PIX - 1) / 2.0
    fibers = trace.shape[0]
    return (jnp.repeat(centre, PIX, axis=1), jnp.repeat(spread, PIX, axis=1), jnp.tile(offsets, fibers))

def lamp_model(lit_row, amp_row, centre, spread, offsets):
    scaled = (offsets[None, :] - centre) / spread
    shape = lit_row[:, None] * amp_row[None, :] * jnp.exp(-0.5 * scaled * scaled)
    return (shape, scaled)

def accumulate(frames, lit, amp_cols, centre, spread, offsets):

    def one_lamp(carry, item):
        frame, lit_row, amp_row = item
        shape, scaled = lamp_model(lit_row, amp_row, centre, spread, offsets)
        resid = frame.astype(jnp.float32) - shape
        slope = shape * scaled / spread
        widen = shape * scaled * scaled
        return ((carry[0] + slope * slope, carry[1] + slope * widen, carry[2] + widen * widen, carry[3] + resid * slope, carry[4] + resid * widen), None)
    zeros = jnp.zeros(centre.shape, jnp.float32)
    sums, _ = lax.scan(one_lamp, (zeros, zeros, zeros, zeros, zeros), (frames, lit, amp_cols))
    rows_here, cols = centre.shape
    return tuple((item.reshape(rows_here, cols // PIX, PIX).sum(axis=2) for item in sums))

def normal_blocks(sums, ptab):
    rows_here = ptab.shape[0]
    pairs = (ptab[:, :, None] * ptab[:, None, :]).reshape(rows_here, K * K)
    fibers = sums[0].shape[1]
    nxx = jnp.dot(sums[0].T, pairs, precision=HIGH).reshape(fibers, K, K)
    nxs = jnp.dot(sums[1].T, pairs, precision=HIGH).reshape(fibers, K, K)
    nss = jnp.dot(sums[2].T, pairs, precision=HIGH).reshape(fibers, K, K)
    upper = jnp.concatenate([nxx, nxs], axis=2)
    lower = jnp.concatenate([jnp.swapaxes(nxs, 1, 2), nss], axis=2)
    normal = jnp.concatenate([upper, lower], axis=1).reshape(fibers, 4 * K * K)
    grad = jnp.concatenate([jnp.dot(sums[3].T, ptab, precision=HIGH), jnp.dot(sums[4].T, ptab, precision=HIGH)], axis=1)
    return (normal, grad)

def solve_step(normal, grad, trace, width):
    fibers = normal.shape[0]
    matrix = normal.reshape(fibers, 2 * K, 2 * K)
    diag_vals = jnp.diagonal(matrix, axis1=1, axis2=2)
    eye_mat = jnp.eye(2 * K, dtype=jnp.float32)
    matrix = matrix + (0.5 * diag_vals + 1.0)[:, :, None] * eye_mat[None, :, :]
    factor = jnp.linalg.cholesky(matrix)
    inner = jax.scipy.linalg.solve_triangular(factor, grad[:, :, None], lower=True)
    update = jax.scipy.linalg.solve_triangular(factor, inner, lower=True, trans=1)[:, :, 0]
    return (trace + update[:, :K], width + update[:, K:])

def residual_image(frames, lit, amp_cols, centre, spread, offsets):

    def one_lamp(item):
        frame, lit_row, amp_row = item
        shape, scaled = lamp_model(lit_row, amp_row, centre, spread, offsets)
        return (frame.astype(jnp.float32) - shape).astype(jnp.bfloat16)
    return lax.map(one_lamp, (frames, lit, amp_cols))

def reference(frames, amplitude, line_start, bundle_width, fiber_bundle, trace_coef, width_coef):
    nrow = frames.shape[1]
    ptab = legendre_table(0, nrow, nrow)
    lit = lit_rows(line_start, 0, nrow)
    amp_cols = jnp.repeat(amplitude, PIX, axis=1)
    trace, width = (trace_coef, width_coef)
    for step in range(ITERS):
        centre, spread, offsets = profile_cols(trace, width, bundle_width, fiber_bundle, ptab)
        sums = accumulate(frames, lit, amp_cols, centre, spread, offsets)
        normal, grad = normal_blocks(sums, ptab)
        trace, width = solve_step(normal, grad, trace, width)
    centre, spread, offsets = profile_cols(trace, width, bundle_width, fiber_bundle, ptab)
    return (trace, width, residual_image(frames, lit, amp_cols, centre, spread, offsets))
```

```python
import functools
import math

import jax
import jax.numpy as jnp
import numpy as np
from jax import lax
from jax.experimental import pallas as pl
from jax.experimental.pallas import tpu as pltpu
from jax.sharding import PartitionSpec as P

K = 11
PIX = 8
WIN = 8
ITERS = 3
LANES = 128
NDEV = 128
PLANES = 4
PER = 32
MINE = 4
SLOT = 32
KAPPA = math.sqrt(0.5 / math.log(2.0))
F32 = jnp.float32
BF16 = jnp.bfloat16
MESH = pl.DeviceIdType.MESH
HIGH = lax.Precision.HIGHEST


def adams_factor(order):
    value = 1.0
    for index in range(1, order + 1):
        value = value * (2.0 * index - 1.0) / index
    return value


def product_table():
    table = np.zeros((2 * K - 1, K, K))
    for a in range(K):
        for b in range(K):
            for m in range(min(a, b) + 1):
                target = a + b - 2 * m
                weight = adams_factor(m) * adams_factor(a - m) * adams_factor(b - m)
                weight = weight / adams_factor(a + b - m)
                weight = weight * (2.0 * target + 1.0) / (2.0 * (a + b - m) + 1.0)
                table[target, a, b] += weight
    return table


MOMENTS = 2 * K - 1
GRAD0 = 3 * MOMENTS


def link_table():
    link = product_table()
    out = np.zeros((LANES, 24 * SLOT))
    for i in range(2 * K):
        for k in range(2 * K):
            which = (i >= K) + (k >= K)
            damp = 1.5 if i == k else 1.0
            out[which * MOMENTS : (which + 1) * MOMENTS, i * SLOT + k] = damp * link[:, i % K, k % K]
        out[GRAD0 + i, i * SLOT + 2 * K] = 1.0
    high = jnp.asarray(out, F32).astype(BF16)
    low = (jnp.asarray(out, F32) - high.astype(F32)).astype(BF16)
    return jnp.concatenate([high, low], axis=0)


def iota(shape, dim):
    return lax.broadcasted_iota(jnp.int32, shape, dim)


def legendre(t, count):
    polys = [jnp.ones_like(t), t]
    for n in range(1, count - 1):
        polys.append(((2 * n + 1) * t * polys[n] - n * polys[n - 1]) / (n + 1))
    return polys[:count]


def t_of(row, total):
    return (2.0 * row.astype(F32) + 1.0) / total - 1.0


def split(x):
    high = x.astype(BF16)
    return high, (x - high.astype(F32)).astype(BF16)


def lit_row(starts, lamp, lines, first):
    row = first + iota((1, LANES), 1)
    hit = jnp.zeros((1, LANES), F32)
    for i in range(lines):
        low = starts[lamp, i]
        hit = jnp.where((row >= low) & (row < low + WIN), 1.0, hit)
    return hit


def base_row(fiber_bundle, bundle_width, bundles):
    out = jnp.zeros(fiber_bundle.shape, F32)
    for b in range(bundles):
        out = jnp.where(fiber_bundle == b, bundle_width[b], out)
    return out


def fit_kernel(
    lamps, lines, bundles, nrow,
    starts, bundle_width, fiber_bundle, amplitude, trace, width, link_hbm, frames_hbm,
    out,
    frames, ft, fq, a2, invb, mix, litc, px, tb, xq, whi, wlo, link, row, ag, mom, rs,
    in_sem, link_sem, ag_send, ag_recv, rs_send, rs_recv,
):
    my_row, my_fib = lax.axis_index("rows"), lax.axis_index("fib")
    me = my_row * 4 + my_fib
    my_z, my_in = me // PER, me % PER
    first = my_row * LANES

    for lamp in range(lamps):
        pltpu.make_async_copy(frames_hbm.at[lamp], frames.at[lamp], in_sem.at[lamp]).start()
    pltpu.make_async_copy(link_hbm, link, link_sem).start()

    barrier = pltpu.get_barrier_semaphore()

    @pl.loop(1, NDEV)
    def _(i):
        peer = (me + i) % NDEV
        pl.semaphore_signal(barrier, inc=1, device_id=(peer // 4, peer % 4), device_id_type=MESH)

    def tell_everyone(step):
        pltpu.make_async_copy(row.at[step], ag.at[step, me], ag_recv.at[step, my_z]).start()

        @pl.loop(1, NDEV)
        def _(i):
            peer = (me + i) % NDEV
            pltpu.make_async_remote_copy(
                src_ref=row.at[step],
                dst_ref=ag.at[step, me],
                send_sem=ag_send.at[step],
                recv_sem=ag_recv.at[step, my_z],
                device_id=(peer // 4, peer % 4),
                device_id_type=MESH,
            ).start()

    row[0] = jnp.zeros((1, LANES), F32)
    for j in range(MINE):
        row[0, :, SLOT * j : SLOT * j + K] = trace[j : j + 1, :]
        row[0, :, SLOT * j + K : SLOT * j + 2 * K] = width[j : j + 1, :]

    px[...] = jnp.zeros(px.shape, BF16)
    sub = iota((SLOT, LANES), 0)
    polys = legendre(t_of(first + iota((1, LANES), 1), nrow), K)
    for part in range(2):
        table = jnp.zeros((SLOT, LANES), F32)
        for k in range(K):
            table = jnp.where(sub == k + part * K, (1.0, -1.0)[part] * polys[k], table)
        high, low = split(table)
        for j in range(MINE):
            lanes = pl.ds((2 * j + part) * LANES, LANES)
            px[pl.ds(SLOT * j, SLOT), lanes] = high
            px[pl.ds(LANES + SLOT * j, SLOT), lanes] = low

    @pl.loop(0, LANES // 16)
    def _(b):
        lane = iota((16, LANES), 1)
        degree = jnp.where(lane < GRAD0, lane % MOMENTS, (lane - GRAD0) % K)
        degree = jnp.where(lane < GRAD0 + 2 * K, degree, -1)
        wide = legendre(t_of(first + b * 16 + iota((16, LANES), 0), nrow), MOMENTS)
        table = jnp.zeros((16, LANES), F32)
        for k in range(MOMENTS):
            table = jnp.where(degree == k, wide[k], table)
        table = table * jnp.where(lane < GRAD0, KAPPA**-4, KAPPA**-2)
        ends = [0, MOMENTS, 2 * MOMENTS, GRAD0, GRAD0 + K, GRAD0 + 2 * K]
        for a in range(5):
            inside = (lane >= ends[a]) & (lane < ends[a + 1])
            high, low = split(jnp.where(inside, table, 0.0))
            rows = pl.ds(pl.multiple_of(a * LANES + b * 16, 16), 16)
            tb[rows, 0:LANES] = high
            tb[rows, LANES : 2 * LANES] = low

    pl.semaphore_wait(barrier, NDEV - 1)
    tell_everyone(0)

    lits = [lit_row(starts, lamp, lines, first) for lamp in range(lamps)]
    for lamp in range(lamps):
        litc[lamp] = jnp.transpose(jnp.broadcast_to(lits[lamp], (LANES, LANES)))
    base = base_row(fiber_bundle[...], bundle_width, bundles)
    sub8 = iota((8, LANES), 0)
    sub8w = iota((8, amplitude.shape[1]), 0)
    amp = jnp.zeros(sub8w.shape, F32)
    lit8 = jnp.zeros((8, LANES), F32)
    for lamp in range(lamps):
        amp = jnp.where(sub8w == lamp, amplitude[lamp : lamp + 1, :], amp)
        lit8 = jnp.where(sub8 == lamp, lits[lamp], lit8)
    left = jnp.where(sub8w == lamps, KAPPA / base, amp * amp)
    right = jnp.concatenate([lit8, jnp.where(sub8 == lamps, 1.0, jnp.zeros((8, LANES), F32))], axis=1)
    mixed = lax.dot_general(
        jnp.transpose(left), right, (((1,), (0,)), ((), ())), precision=HIGH, preferred_element_type=F32
    )
    for part, dest in enumerate((a2, invb)):
        mix[...] = mixed[:, part * LANES : (part + 1) * LANES]
        for j in range(MINE):
            dest[j] = mix[pl.ds(j, NDEV, stride=MINE), :]

    for lamp in range(lamps):
        pltpu.make_async_copy(frames_hbm.at[lamp], frames.at[lamp], in_sem.at[lamp]).wait()
    spread = iota((8, LANES), 1) // PIX
    for b in range(32):
        cols = pl.ds(b * LANES, LANES)
        part = lax.slice_in_dim(amp, (b // 8) * LANES, (b // 8 + 1) * LANES, axis=1)
        bright = jnp.take_along_axis(part, spread + 16 * (b % 8), axis=1)
        total = jnp.zeros((LANES, LANES), F32)
        for lamp in range(lamps):
            weight = litc[lamp] * bright[lamp : lamp + 1, :]
            total = total + weight * frames[lamp, :, cols].astype(F32)
        ft[pl.ds(b * LANES, LANES), :] = jnp.transpose(total)

    @pl.loop(0, 32)
    def _(q):
        fq[q] = ft[pl.ds(q, NDEV, stride=32), :]

    pltpu.make_async_copy(link_hbm, link, link_sem).wait()

    def one_plane(step, hop):
        z = (my_z + hop) % PLANES
        d0 = pl.multiple_of(z * PER, PER)
        here = ag.at[step, pl.ds(d0, PER)]
        pltpu.make_async_copy(here, here, ag_recv.at[step, z]).wait()
        coef = ag[step, pl.ds(d0, PER), 0, :]
        high, low = split(coef)
        lhs = jnp.concatenate(
            [jnp.concatenate([high, high], axis=1), jnp.concatenate([low, low], axis=1)], axis=0
        )
        both = jnp.dot(lhs, px[...], preferred_element_type=F32)
        xq[...] = both[0:PER] + both[PER : 2 * PER]

        for j in range(MINE):
            for half in range(2):
                rows = pl.ds(half * 16, 16)
                drows = pl.ds(pl.multiple_of(d0 + half * 16, 16), 16)
                x = xq[rows, (2 * j) * LANES : (2 * j + 1) * LANES]
                inv = jnp.exp(xq[rows, (2 * j + 1) * LANES : (2 * j + 2) * LANES]) * invb[j, drows, :]
                bright2 = a2[j, drows, :]
                sxx = sxs = sss = hx = hs = jnp.zeros((16, LANES), F32)
                for p in range(PIX):
                    u = ((p - (PIX - 1) / 2.0) - x) * inv
                    g = jnp.exp2(-(u * u))
                    gu = g * u
                    m = gu * gu
                    n = m * u
                    tg = (fq[PIX * j + p, drows, :] - bright2 * g) * gu
                    sxx = sxx + m
                    sxs = sxs + n
                    sss = sss + n * u
                    hx = hx + tg
                    hs = hs + tg * u
                binv = bright2 * inv
                sums = (binv * inv * sxx, binv * sxs, bright2 * sss, inv * hx, hs)
                wrows = pl.ds(j * PER + half * 16, 16)
                for a in range(5):
                    h, l = split(sums[a])
                    whi[wrows, a * LANES : (a + 1) * LANES] = h
                    wlo[wrows, a * LANES : (a + 1) * LANES] = l
        one = jnp.dot(whi[...], tb[...], preferred_element_type=F32)
        two = jnp.dot(wlo[...], tb[:, 0:LANES], preferred_element_type=F32)
        moments = one[:, 0:LANES] + one[:, LANES : 2 * LANES] + two
        for j in range(MINE):
            mom[step, pl.ds(d0, PER), j, :] = moments[j * PER : (j + 1) * PER, :]

        @pl.loop(1 if hop == 0 else 0, PER)
        def _(i):
            peer = d0 + (my_in + i) % PER
            pltpu.make_async_remote_copy(
                src_ref=mom.at[step, peer],
                dst_ref=rs.at[step, me],
                send_sem=rs_send.at[step],
                recv_sem=rs_recv.at[step],
                device_id=(peer // 4, peer % 4),
                device_id_type=MESH,
            ).start()

        if hop == 0:
            pltpu.make_async_copy(mom.at[step, me], rs.at[step, me], rs_recv.at[step]).start()

    def solve(step):
        pltpu.make_async_copy(rs.at[step], rs.at[step], rs_recv.at[step]).wait()
        parts = [rs[step, pl.ds(32 * i, 32)].sum(axis=0) for i in range(4)]
        total = (parts[0] + parts[1]) + (parts[2] + parts[3])
        high = total.astype(BF16).astype(F32)
        both = jnp.concatenate([high, total - high], axis=0)
        lhs = jnp.concatenate([both, both], axis=1).astype(BF16)
        both = jnp.dot(lhs, link[...], preferred_element_type=F32)
        both = both[0:MINE] + both[MINE : 2 * MINE]
        lane = iota((MINE, LANES), 1)
        system = []
        for i in range(2 * K):
            block = both[:, (i // 4) * LANES : (i // 4 + 1) * LANES]
            if i % 4:
                block = pltpu.roll(block, LANES - SLOT * (i % 4), axis=1)
            system.append(jnp.where(lane == i, block + 1.0, block))
        for k in range(2 * K):
            scaled = system[k] * (1.0 / system[k][:, k : k + 1])
            for i in range(2 * K):
                if i != k:
                    system[i] = system[i] - system[i][:, k : k + 1] * scaled
            system[k] = scaled
        found = jnp.zeros((MINE, LANES), F32)
        for i in range(2 * K):
            found = jnp.where(lane % SLOT == i, system[i][:, 2 * K : 2 * K + 1], found)
        found = jnp.where(iota((MINE, LANES), 0) == lane // SLOT, found, 0.0)
        row[step + 1] = row[step] + found.sum(axis=0, keepdims=True)

    @pl.loop(0, ITERS)
    def _(step):
        for hop in (0, 1, 3, 2):
            one_plane(step, hop)
        solve(step)
        tell_everyone(step + 1)
        sent = mom.at[step, pl.ds(0, NDEV - 1)]
        pltpu.make_async_copy(sent, sent, rs_send.at[step]).wait()
        told = ag.at[step, pl.ds(0, NDEV - 1)]
        pltpu.make_async_copy(told, told, ag_send.at[step]).wait()

    for z in range(PLANES):
        here = ag.at[ITERS, pl.ds(z * PER, PER)]
        pltpu.make_async_copy(here, here, ag_recv.at[ITERS, z]).wait()
    out[...] = ag[ITERS, :, 0, :]
    told = ag.at[ITERS, pl.ds(0, NDEV - 1)]
    pltpu.make_async_copy(told, told, ag_send.at[ITERS]).wait()


def fit(starts, bundle_width, fiber_bundle, amplitude, trace, width, frames, nrow):
    lamps, rows, cols = frames.shape
    vmem = pl.BlockSpec(memory_space=pltpu.VMEM)
    smem = pl.BlockSpec(memory_space=pltpu.SMEM)
    hbm = pl.BlockSpec(memory_space=pl.ANY)
    dma = pltpu.SemaphoreType.DMA
    kernel = functools.partial(fit_kernel, lamps, starts.shape[1], bundle_width.shape[0], nrow)
    return pl.pallas_call(
        kernel,
        out_shape=jax.ShapeDtypeStruct((NDEV, LANES), F32),
        in_specs=[smem, smem, vmem, vmem, vmem, vmem, hbm, hbm],
        out_specs=vmem,
        scratch_shapes=[
            pltpu.VMEM((lamps, rows, cols), BF16),
            pltpu.VMEM((cols, LANES), F32),
            pltpu.VMEM((32, NDEV, LANES), F32),
            pltpu.VMEM((MINE, NDEV, LANES), F32),
            pltpu.VMEM((MINE, NDEV, LANES), F32),
            pltpu.VMEM((MINE * NDEV, LANES), F32),
            pltpu.VMEM((lamps, LANES, LANES), F32),
            pltpu.VMEM((2 * LANES, 8 * LANES), BF16),
            pltpu.VMEM((5 * LANES, 2 * LANES), BF16),
            pltpu.VMEM((PER, 8 * LANES), F32),
            pltpu.VMEM((LANES, 5 * LANES), BF16),
            pltpu.VMEM((LANES, 5 * LANES), BF16),
            pltpu.VMEM((2 * LANES, 24 * SLOT), BF16),
            pltpu.VMEM((ITERS + 1, 1, LANES), F32),
            pltpu.VMEM((ITERS + 1, NDEV, 1, LANES), F32),
            pltpu.VMEM((ITERS, NDEV, MINE, LANES), F32),
            pltpu.VMEM((ITERS, NDEV, MINE, LANES), F32),
            dma((lamps,)),
            dma,
            dma((ITERS + 1,)),
            dma((ITERS + 1, PLANES)),
            dma((ITERS,)),
            dma((ITERS,)),
        ],
        compiler_params=pltpu.CompilerParams(
            collective_id=0, has_side_effects=True, vmem_limit_bytes=40 << 20
        ),
        name="fit",
    )(starts, bundle_width, fiber_bundle, amplitude, trace, width, link_table(), frames)


def residual_kernel(
    lamps, lines, bundles, nrow,
    starts, bundle_width, fiber_bundle, amplitude, coef, frames,
    trace_out, width_out, out,
    table, rates, litc, ptab,
):
    my_row = lax.axis_index("rows")
    me = my_row * 4 + lax.axis_index("fib")
    first = my_row * LANES
    step = pl.program_id(0)
    wide = frames.shape[2]

    @pl.when(step == 0)
    def _():
        mine = coef[pl.ds(me, 1), :]
        for j in range(MINE):
            trace_out[j : j + 1, :] = mine[:, SLOT * j : SLOT * j + K]
            width_out[j : j + 1, :] = mine[:, SLOT * j + K : SLOT * j + 2 * K]
        for lamp in range(lamps):
            litc[lamp] = jnp.transpose(
                jnp.broadcast_to(lit_row(starts, lamp, lines, first), (LANES, LANES))
            )
        lane = iota((LANES, LANES), 1)
        polys = legendre(t_of(first + iota((LANES, LANES), 0), nrow), K)
        for part in range(2):
            tab = jnp.zeros((LANES, LANES), F32)
            for k in range(K):
                tab = jnp.where(lane % SLOT == k + part * K, (1.0, -1.0)[part] * polys[k], tab)
            high = tab.astype(BF16).astype(F32)
            tab = jnp.where(lane < 2 * SLOT, high, jnp.where(lane < 3 * SLOT, tab - high, 0.0))
            ptab[pl.ds(part * LANES, LANES), :] = tab.astype(BF16)
        base = base_row(fiber_bundle[...], bundle_width, bundles)
        fibers = fiber_bundle.shape[1]
        sub8w = iota((8, fibers), 0)
        rate = jnp.broadcast_to(KAPPA / base, (8, fibers))
        for lamp in range(lamps):
            rate = jnp.where(sub8w == lamp, amplitude[lamp : lamp + 1, :], rate)
        turned = jnp.transpose(coef[...])
        lane = iota((SLOT, LANES), 1)
        lane8 = iota((8, LANES), 1) // PIX
        for fb in range(4):
            pick = 32 * fb + lane // MINE
            named = jnp.zeros((SLOT, LANES), F32)
            for j in range(MINE):
                got = jnp.take_along_axis(turned[SLOT * j : SLOT * (j + 1), :], pick, axis=1)
                named = jnp.where(lane % MINE == j, got, named)
            part = rate[:, fb * LANES : (fb + 1) * LANES]
            for b in range(8):
                cols = pl.ds((8 * fb + b) * LANES, LANES)
                got = jnp.take_along_axis(named, lane // PIX + 16 * b, axis=1)
                high, low = split(got)
                table[0:SLOT, cols] = high
                table[SLOT : 2 * SLOT, cols] = low
                table[2 * SLOT : 3 * SLOT, cols] = high
                table[3 * SLOT : 4 * SLOT, cols] = jnp.zeros((SLOT, LANES), BF16)
                rates[:, cols] = jnp.take_along_axis(part, lane8 + 16 * b, axis=1)

    offset = (iota((1, LANES), 1) % PIX).astype(F32) - (PIX - 1) / 2.0
    here = pl.ds(pl.multiple_of(step * wide, LANES), wide)
    xq = jnp.dot(ptab[...], table[:, here], preferred_element_type=F32)
    rate = rates[:, here]
    for b in range(wide // LANES):
        cols = slice(b * LANES, (b + 1) * LANES)
        x, q = xq[0:LANES, cols], xq[LANES : 2 * LANES, cols]
        u = (offset - x) * (jnp.exp(q) * rate[lamps : lamps + 1, cols])
        g = jnp.exp2(-(u * u))
        for lamp in range(lamps):
            model = (litc[lamp] * rate[lamp : lamp + 1, cols]) * g
            out[lamp, :, cols] = (frames[lamp, :, cols].astype(F32) - model).astype(BF16)


def residual(starts, bundle_width, fiber_bundle, amplitude, coef, frames, nrow):
    lamps, rows, cols = frames.shape
    wide = 512
    vmem = pl.BlockSpec(memory_space=pltpu.VMEM)
    smem = pl.BlockSpec(memory_space=pltpu.SMEM)
    strip = pl.BlockSpec((lamps, rows, wide), lambda i: (0, 0, i))
    kernel = functools.partial(residual_kernel, lamps, starts.shape[1], bundle_width.shape[0], nrow)
    small = jax.ShapeDtypeStruct((MINE, K), F32)
    return pl.pallas_call(
        kernel,
        grid=(cols // wide,),
        out_shape=(small, small, jax.ShapeDtypeStruct(frames.shape, BF16)),
        in_specs=[smem, smem, vmem, vmem, vmem, strip],
        out_specs=(vmem, vmem, strip),
        scratch_shapes=[
            pltpu.VMEM((LANES, cols), BF16),
            pltpu.VMEM((8, cols), F32),
            pltpu.VMEM((lamps, LANES, LANES), F32),
            pltpu.VMEM((2 * LANES, LANES), BF16),
        ],
        compiler_params=pltpu.CompilerParams(vmem_limit_bytes=30 << 20),
        name="residual",
    )(starts, bundle_width, fiber_bundle, amplitude, coef, frames)


def body(frames, amplitude, line_start, bundle_width, fiber_bundle, trace_coef, width_coef):
    nrow = frames.shape[1] * lax.axis_size("rows")
    bundle = fiber_bundle.reshape(1, -1)
    coef = fit(line_start, bundle_width, bundle, amplitude, trace_coef, width_coef, frames, nrow)
    return residual(line_start, bundle_width, bundle, amplitude, coef, frames, nrow)


def solution(mesh):
    placed = (
        P("fib", "rows", None),
        P("fib", None),
        P("fib", None),
        P(),
        P(),
        P(("rows", "fib"), None),
        P(("rows", "fib"), None),
    )
    return jax.shard_map(
        body,
        mesh=mesh,
        in_specs=placed,
        out_specs=(P(("rows", "fib"), None), P(("rows", "fib"), None), P("fib", "rows", None)),
        check_vma=False,
    )
```

```python
import functools
import itertools
import math

import jax
import jax.numpy as jnp
import numpy as np
from jax import lax
from jax.experimental import pallas as pl
from jax.experimental.pallas import tpu as pltpu
from jax.sharding import PartitionSpec as P

K = 11
PIX = 8
WIN = 8
ITERS = 3
LANES = 128
NDEV = 128
PLANES = 4
PER = 32
MINE = 4
SLOT = 32
KAPPA = math.sqrt(0.5 / math.log(2.0))
F32 = jnp.float32
BF16 = jnp.bfloat16
MESH = pl.DeviceIdType.MESH
HIGH = lax.Precision.HIGHEST


def adams_factor(order):
    value = 1.0
    for index in range(1, order + 1):
        value = value * (2.0 * index - 1.0) / index
    return value


def product_table():
    table = np.zeros((2 * K - 1, K, K))
    for a in range(K):
        for b in range(K):
            for m in range(min(a, b) + 1):
                target = a + b - 2 * m
                weight = adams_factor(m) * adams_factor(a - m) * adams_factor(b - m)
                weight = weight / adams_factor(a + b - m)
                weight = weight * (2.0 * target + 1.0) / (2.0 * (a + b - m) + 1.0)
                table[target, a, b] += weight
    return table


MOMENTS = 2 * K - 1
GRAD0 = 3 * MOMENTS


def link_table():
    link = product_table()
    out = np.zeros((LANES, 24 * SLOT))
    for i in range(2 * K):
        for k in range(2 * K):
            which = (i >= K) + (k >= K)
            damp = 1.5 if i == k else 1.0
            out[which * MOMENTS : (which + 1) * MOMENTS, i * SLOT + k] = damp * link[:, i % K, k % K]
        out[GRAD0 + i, i * SLOT + 2 * K] = 1.0
    high = jnp.asarray(out, F32).astype(BF16)
    low = (jnp.asarray(out, F32) - high.astype(F32)).astype(BF16)
    return jnp.concatenate([high, low], axis=0)


def iota(shape, dim):
    return lax.broadcasted_iota(jnp.int32, shape, dim)


def legendre(t, count):
    polys = [jnp.ones_like(t), t]
    for n in range(1, count - 1):
        polys.append(((2 * n + 1) * t * polys[n] - n * polys[n - 1]) / (n + 1))
    return polys[:count]


def t_of(row, total):
    return (2.0 * row.astype(F32) + 1.0) / total - 1.0


def split(x):
    high = x.astype(BF16)
    return high, (x - high.astype(F32)).astype(BF16)


def lit_row(starts, lamp, lines, first):
    row = first + iota((1, LANES), 1)
    hit = jnp.zeros((1, LANES), F32)
    for i in range(lines):
        low = starts[lamp, i]
        hit = jnp.where((row >= low) & (row < low + WIN), 1.0, hit)
    return hit


def base_row(fiber_bundle, bundle_width, bundles):
    out = jnp.zeros(fiber_bundle.shape, F32)
    for b in range(bundles):
        out = jnp.where(fiber_bundle == b, bundle_width[b], out)
    return out


def offsets():
    every = itertools.product(range(PLANES), range(4), range(2), range(4))
    hops = lambda o: sum(min(o[i], 4 - o[i]) for i in (0, 1, 3))
    return sorted((o for o in every if any(o)), key=lambda o: (-hops(o), o[2]))


def fit_kernel(
    lamps, lines, bundles, nrow,
    starts_hbm, bundle_hbm, fiber_hbm, amp_hbm, trace_hbm, width_hbm, link_hbm, frames_hbm,
    out, rates, litc, flags, ptab,
    starts, bundle_width, fiber_bundle, amplitude, trace, width,
    frames, ft, fq, a2, invb, mix, px, tb, xq, whi, wlo, link, row, ag, mom, rs,
    in_sem, small_sem, link_sem, ag_send, ag_recv, rs_send, rs_recv,
):
    my_row, my_fib = lax.axis_index("rows"), lax.axis_index("fib")
    me = my_row * 4 + my_fib
    my_z, my_y, my_core = my_row // 8, (my_row // 2) % 4, my_row % 2
    first = my_row * LANES
    zs = [(my_z + i) % PLANES for i in range(PLANES)]
    ys = [(my_y + i) % 4 for i in range(4)]
    cores = [my_core, 1 - my_core]
    fibs = [(my_fib + i) % 4 for i in range(4)]
    inner = {(y, c): ys[y] * 2 + cores[c] for y in range(4) for c in range(2)}
    rows_of = {(z, y, c): zs[z] * 8 + inner[y, c] for z in range(PLANES) for y, c in inner}

    barrier = pltpu.get_barrier_semaphore()
    for off in offsets():
        peer = (rows_of[off[:3]], fibs[off[3]])
        pl.semaphore_signal(barrier, inc=1, device_id=peer, device_id_type=MESH)

    small = [
        pltpu.make_async_copy(a, b, small_sem.at[i])
        for i, (a, b) in enumerate(
            (
                (trace_hbm, trace),
                (width_hbm, width),
                (starts_hbm, starts),
                (bundle_hbm, bundle_width),
                (fiber_hbm, fiber_bundle),
                (amp_hbm, amplitude),
            )
        )
    ]
    for copy in small:
        copy.start()
    for lamp in range(lamps):
        pltpu.make_async_copy(frames_hbm.at[lamp], frames.at[lamp], in_sem.at[lamp]).start()
    pltpu.make_async_copy(link_hbm, link, link_sem).start()

    def tell_everyone(step):
        for off in offsets():
            pltpu.make_async_remote_copy(
                src_ref=row.at[step],
                dst_ref=ag.at[step, me],
                send_sem=ag_send.at[step],
                recv_sem=ag_recv.at[step, my_z],
                device_id=(rows_of[off[:3]], fibs[off[3]]),
                device_id_type=MESH,
            ).start()
        pltpu.make_async_copy(row.at[step], ag.at[step, me], ag_recv.at[step, my_z]).start()

    for copy in small:
        copy.wait()

    row[0] = jnp.zeros((1, LANES), F32)
    for j in range(MINE):
        row[0, :, SLOT * j : SLOT * j + K] = trace[j : j + 1, :]
        row[0, :, SLOT * j + K : SLOT * j + 2 * K] = width[j : j + 1, :]

    px[...] = jnp.zeros(px.shape, BF16)
    sub = iota((SLOT, LANES), 0)
    polys = legendre(t_of(first + iota((1, LANES), 1), nrow), K)
    for part in range(2):
        table = jnp.zeros((SLOT, LANES), F32)
        for k in range(K):
            table = jnp.where(sub == k + part * K, (1.0, -1.0)[part] * polys[k], table)
        high, low = split(table)
        for j in range(MINE):
            lanes = pl.ds((2 * j + part) * LANES, LANES)
            px[pl.ds(SLOT * j, SLOT), lanes] = high
            px[pl.ds(LANES + SLOT * j, SLOT), lanes] = low

    @pl.loop(0, LANES // 16)
    def _(b):
        lane = iota((16, LANES), 1)
        degree = jnp.where(lane < GRAD0, lane % MOMENTS, (lane - GRAD0) % K)
        degree = jnp.where(lane < GRAD0 + 2 * K, degree, -1)
        wide = legendre(t_of(first + b * 16 + iota((16, LANES), 0), nrow), MOMENTS)
        table = jnp.zeros((16, LANES), F32)
        for k in range(MOMENTS):
            table = jnp.where(degree == k, wide[k], table)
        table = table * jnp.where(lane < GRAD0, KAPPA**-4, KAPPA**-2)
        ends = [0, MOMENTS, 2 * MOMENTS, GRAD0, GRAD0 + K, GRAD0 + 2 * K]
        for a in range(5):
            inside = (lane >= ends[a]) & (lane < ends[a + 1])
            high, low = split(jnp.where(inside, table, 0.0))
            rows = pl.ds(pl.multiple_of(a * LANES + b * 16, 16), 16)
            tb[rows, 0:LANES] = high
            tb[rows, LANES : 2 * LANES] = low

    @pl.loop(0, LANES // 16)
    def _(b):
        lane = iota((16, LANES), 1)
        polys = legendre(t_of(first + b * 16 + iota((16, LANES), 0), nrow), K)
        for part in range(2):
            table = jnp.zeros((16, LANES), F32)
            for k in range(K):
                table = jnp.where(lane % SLOT == k + part * K, (1.0, -1.0)[part] * polys[k], table)
            high = table.astype(BF16).astype(F32)
            table = jnp.where(lane < 2 * SLOT, high, jnp.where(lane < 3 * SLOT, table - high, 0.0))
            rows = pl.ds(pl.multiple_of(part * LANES + b * 16, 16), 16)
            ptab[rows, :] = table.astype(BF16)

    pl.semaphore_wait(barrier, NDEV - 1)
    tell_everyone(0)

    lits = [lit_row(starts, lamp, lines, first) for lamp in range(lamps)]
    for lamp in range(lamps):
        litc[lamp] = jnp.transpose(jnp.broadcast_to(lits[lamp], (LANES, LANES)))
    base = base_row(fiber_bundle[...], bundle_width, bundles)
    sub8 = iota((8, LANES), 0)
    sub8w = iota((8, amplitude.shape[1]), 0)
    amp = jnp.zeros(sub8w.shape, F32)
    lit8 = jnp.zeros((8, LANES), F32)
    for lamp in range(lamps):
        amp = jnp.where(sub8w == lamp, amplitude[lamp : lamp + 1, :], amp)
        lit8 = jnp.where(sub8 == lamp, lits[lamp], lit8)
    blocks = (iota((LANES, LANES), 0) // 16 == iota((LANES, LANES), 1)).astype(F32)
    flags[...] = jnp.dot(lit8, blocks, preferred_element_type=F32).astype(jnp.int32)
    left = jnp.where(sub8w == lamps, KAPPA / base, amp * amp)
    right = jnp.concatenate([lit8, jnp.where(sub8 == lamps, 1.0, jnp.zeros((8, LANES), F32))], axis=1)
    mixed = lax.dot_general(
        jnp.transpose(left), right, (((1,), (0,)), ((), ())), precision=HIGH, preferred_element_type=F32
    )
    for part, dest in enumerate((a2, invb)):
        mix[...] = mixed[:, part * LANES : (part + 1) * LANES]
        for j in range(MINE):
            dest[j] = mix[pl.ds(j, NDEV, stride=MINE), :]

    for lamp in range(lamps):
        pltpu.make_async_copy(frames_hbm.at[lamp], frames.at[lamp], in_sem.at[lamp]).wait()
    spread = iota((8, LANES), 1) // PIX
    rate = jnp.where(sub8w == lamps, KAPPA / base, amp)
    for b in range(32):
        cols = pl.ds(b * LANES, LANES)
        part = lax.slice_in_dim(amp, (b // 8) * LANES, (b // 8 + 1) * LANES, axis=1)
        bright = jnp.take_along_axis(part, spread + 16 * (b % 8), axis=1)
        part = lax.slice_in_dim(rate, (b // 8) * LANES, (b // 8 + 1) * LANES, axis=1)
        rates[:, cols] = jnp.take_along_axis(part, spread + 16 * (b % 8), axis=1)
        total = jnp.zeros((LANES, LANES), F32)
        for lamp in range(lamps):
            weight = litc[lamp] * bright[lamp : lamp + 1, :]
            total = total + weight * frames[lamp, :, cols].astype(F32)
        ft[pl.ds(b * LANES, LANES), :] = jnp.transpose(total)

    @pl.loop(0, 32)
    def _(q):
        fq[q] = ft[pl.ds(q, NDEV, stride=32), :]

    pltpu.make_async_copy(link_hbm, link, link_sem).wait()

    def one_plane(step, hop):
        z = zs[hop]
        d0 = pl.multiple_of(z * PER, PER)
        here = ag.at[step, pl.ds(d0, PER)]
        pltpu.make_async_copy(here, here, ag_recv.at[step, z]).wait()
        coef = ag[step, pl.ds(d0, PER), 0, :]
        high, low = split(coef)
        lhs = jnp.concatenate(
            [jnp.concatenate([high, high], axis=1), jnp.concatenate([low, low], axis=1)], axis=0
        )
        both = jnp.dot(lhs, px[...], preferred_element_type=F32)
        xq[...] = both[0:PER] + both[PER : 2 * PER]

        for j in range(MINE):
            for half in range(2):
                rows = pl.ds(half * 16, 16)
                drows = pl.ds(pl.multiple_of(d0 + half * 16, 16), 16)
                x = xq[rows, (2 * j) * LANES : (2 * j + 1) * LANES]
                inv = jnp.exp(xq[rows, (2 * j + 1) * LANES : (2 * j + 2) * LANES]) * invb[j, drows, :]
                bright2 = a2[j, drows, :]
                sxx = sxs = sss = hx = hs = jnp.zeros((16, LANES), F32)
                for p in range(PIX):
                    u = ((p - (PIX - 1) / 2.0) - x) * inv
                    g = jnp.exp2(-(u * u))
                    gu = g * u
                    m = gu * gu
                    n = m * u
                    tg = (fq[PIX * j + p, drows, :] - bright2 * g) * gu
                    sxx = sxx + m
                    sxs = sxs + n
                    sss = sss + n * u
                    hx = hx + tg
                    hs = hs + tg * u
                binv = bright2 * inv
                sums = (binv * inv * sxx, binv * sxs, bright2 * sss, inv * hx, hs)
                wrows = pl.ds(j * PER + half * 16, 16)
                for a in range(5):
                    h, l = split(sums[a])
                    whi[wrows, a * LANES : (a + 1) * LANES] = h
                    wlo[wrows, a * LANES : (a + 1) * LANES] = l
        one = jnp.dot(whi[...], tb[...], preferred_element_type=F32)
        two = jnp.dot(wlo[...], tb[:, 0:LANES], preferred_element_type=F32)
        moments = one[:, 0:LANES] + one[:, LANES : 2 * LANES] + two
        for j in range(MINE):
            mom[step, pl.ds(d0, PER), j, :] = moments[j * PER : (j + 1) * PER, :]

        for off in offsets():
            if off[0] == hop:
                peer = (rows_of[off[:3]], fibs[off[3]])
                pltpu.make_async_remote_copy(
                    src_ref=mom.at[step, peer[0] * 4 + peer[1]],
                    dst_ref=rs.at[step, me],
                    send_sem=rs_send.at[step],
                    recv_sem=rs_recv.at[step, my_z],
                    device_id=peer,
                    device_id_type=MESH,
                ).start()
        if hop == 0:
            pltpu.make_async_copy(mom.at[step, me], rs.at[step, me], rs_recv.at[step, my_z]).start()

    def solve(step):
        total = jnp.zeros((MINE, LANES), F32)
        for hop in (0, 1, 3, 2):
            d0 = pl.multiple_of(zs[hop] * PER, PER)
            here = rs.at[step, pl.ds(d0, PER)]
            pltpu.make_async_copy(here, here, rs_recv.at[step, zs[hop]]).wait()
            total = total + rs[step, pl.ds(d0, PER)].sum(axis=0)
        high = total.astype(BF16).astype(F32)
        both = jnp.concatenate([high, total - high], axis=0)
        lhs = jnp.concatenate([both, both], axis=1).astype(BF16)
        both = jnp.dot(lhs, link[...], preferred_element_type=F32)
        both = both[0:MINE] + both[MINE : 2 * MINE]
        lane = iota((MINE, LANES), 1)
        system = []
        for i in range(2 * K):
            block = both[:, (i // 4) * LANES : (i // 4 + 1) * LANES]
            if i % 4:
                block = pltpu.roll(block, LANES - SLOT * (i % 4), axis=1)
            system.append(jnp.where(lane == i, block + 1.0, block))
        for k in range(2 * K):
            scaled = system[k] * (1.0 / system[k][:, k : k + 1])
            for i in range(2 * K):
                if i != k:
                    system[i] = system[i] - system[i][:, k : k + 1] * scaled
            system[k] = scaled
        found = jnp.zeros((MINE, LANES), F32)
        for i in range(2 * K):
            found = jnp.where(lane % SLOT == i, system[i][:, 2 * K : 2 * K + 1], found)
        found = jnp.where(iota((MINE, LANES), 0) == lane // SLOT, found, 0.0)
        row[step + 1] = row[step] + found.sum(axis=0, keepdims=True)

    @pl.loop(0, ITERS)
    def _(step):
        for hop in (0, 1, 3, 2):
            one_plane(step, hop)
        solve(step)
        tell_everyone(step + 1)
        sent = mom.at[step, pl.ds(0, NDEV - 1)]
        pltpu.make_async_copy(sent, sent, rs_send.at[step]).wait()
        told = ag.at[step, pl.ds(0, NDEV - 1)]
        pltpu.make_async_copy(told, told, ag_send.at[step]).wait()

    for z in range(PLANES):
        here = ag.at[ITERS, pl.ds(z * PER, PER)]
        pltpu.make_async_copy(here, here, ag_recv.at[ITERS, z]).wait()
    out[...] = ag[ITERS, :, 0, :]
    told = ag.at[ITERS, pl.ds(0, NDEV - 1)]
    pltpu.make_async_copy(told, told, ag_send.at[ITERS]).wait()


def fit(starts, bundle_width, fiber_bundle, amplitude, trace, width, frames, nrow):
    lamps, rows, cols = frames.shape
    vmem = pl.BlockSpec(memory_space=pltpu.VMEM)
    hbm = pl.BlockSpec(memory_space=pltpu.HBM)
    dma = pltpu.SemaphoreType.DMA
    like = lambda space, x: space(x.shape, x.dtype)
    kernel = functools.partial(fit_kernel, lamps, starts.shape[1], bundle_width.shape[0], nrow)
    shape = jax.ShapeDtypeStruct
    return pl.pallas_call(
        kernel,
        out_shape=(
            shape((NDEV, LANES), F32),
            shape((8, cols), F32),
            shape((lamps, LANES, LANES), F32),
            shape((8, LANES), jnp.int32),
            shape((2 * LANES, LANES), BF16),
        ),
        in_specs=[hbm] * 8,
        out_specs=(vmem,) * 5,
        scratch_shapes=[
            like(pltpu.SMEM, starts),
            like(pltpu.SMEM, bundle_width),
            like(pltpu.VMEM, fiber_bundle),
            like(pltpu.VMEM, amplitude),
            like(pltpu.VMEM, trace),
            like(pltpu.VMEM, width),
            pltpu.VMEM((lamps, rows, cols), BF16),
            pltpu.VMEM((cols, LANES), F32),
            pltpu.VMEM((32, NDEV, LANES), F32),
            pltpu.VMEM((MINE, NDEV, LANES), F32),
            pltpu.VMEM((MINE, NDEV, LANES), F32),
            pltpu.VMEM((MINE * NDEV, LANES), F32),
            pltpu.VMEM((2 * LANES, 8 * LANES), BF16),
            pltpu.VMEM((5 * LANES, 2 * LANES), BF16),
            pltpu.VMEM((PER, 8 * LANES), F32),
            pltpu.VMEM((LANES, 5 * LANES), BF16),
            pltpu.VMEM((LANES, 5 * LANES), BF16),
            pltpu.VMEM((2 * LANES, 24 * SLOT), BF16),
            pltpu.VMEM((ITERS + 1, 1, LANES), F32),
            pltpu.VMEM((ITERS + 1, NDEV, 1, LANES), F32),
            pltpu.VMEM((ITERS, NDEV, MINE, LANES), F32),
            pltpu.VMEM((ITERS, NDEV, MINE, LANES), F32),
            dma((lamps,)),
            dma((6,)),
            dma,
            dma((ITERS + 1,)),
            dma((ITERS + 1, PLANES)),
            dma((ITERS,)),
            dma((ITERS, PLANES)),
        ],
        compiler_params=pltpu.CompilerParams(
            collective_id=0, has_side_effects=True, vmem_limit_bytes=24 << 20
        ),
        name="fit",
    )(
        *(
            pltpu.with_memory_space_constraint(x, pltpu.HBM)
            for x in (starts, bundle_width, fiber_bundle, amplitude, trace, width, link_table(), frames)
        )
    )


BLOCK = 16


def residual_kernel(
    lamps,
    flags, coef, rates, litc, ptab, frames,
    trace_out, width_out, out,
    table, xq, shape, done, sem,
):
    me = lax.axis_index("rows") * 4 + lax.axis_index("fib")
    blocks = frames.shape[1] // BLOCK
    cols = frames.shape[2]

    def at(b):
        return pl.ds(pl.multiple_of(b * BLOCK, BLOCK), BLOCK)

    @pl.loop(0, blocks)
    def _(b):
        for lamp in range(lamps):

            @pl.when(flags[lamp, b] == 0)
            def _():
                pltpu.make_async_copy(frames.at[lamp, at(b)], out.at[lamp, at(b)], sem).start()

    mine = coef[pl.ds(me, 1), :]
    for j in range(MINE):
        trace_out[j : j + 1, :] = mine[:, SLOT * j : SLOT * j + K]
        width_out[j : j + 1, :] = mine[:, SLOT * j + K : SLOT * j + 2 * K]

    turned = jnp.transpose(coef[...])
    lane = iota((SLOT, LANES), 1)
    table[3 * SLOT : 4 * SLOT, :] = jnp.zeros((SLOT, cols), BF16)
    for fb in range(4):
        pick = 32 * fb + lane // MINE
        named = jnp.zeros((SLOT, LANES), F32)
        for j in range(MINE):
            got = jnp.take_along_axis(turned[SLOT * j : SLOT * (j + 1), :], pick, axis=1)
            named = jnp.where(lane % MINE == j, got, named)
        for b in range(8):
            here = pl.ds((8 * fb + b) * LANES, LANES)
            got = jnp.take_along_axis(named, lane // PIX + 16 * b, axis=1)
            high, low = split(got)
            table[0:SLOT, here] = high
            table[SLOT : 2 * SLOT, here] = low
            table[2 * SLOT : 3 * SLOT, here] = high
    xq[...] = jnp.dot(ptab[...], table[...], preferred_element_type=F32)

    offset = (iota((1, LANES), 1) % PIX).astype(F32) - (PIX - 1) / 2.0

    @pl.loop(0, blocks)
    def _(b):
        lit = flags[0, b]
        for lamp in range(1, lamps):
            lit = lit + flags[lamp, b]

        @pl.when(lit > 0)
        def _():
            for i in range(cols // LANES):
                here = slice(i * LANES, (i + 1) * LANES)
                x = xq[at(b), here]
                q = xq[pl.ds(pl.multiple_of(LANES + b * BLOCK, BLOCK), BLOCK), here]
                u = (offset - x) * (jnp.exp(q) * rates[lamps : lamps + 1, here])
                shape[:, here] = jnp.exp2(-(u * u))
            for lamp in range(lamps):

                @pl.when(flags[lamp, b] > 0)
                def _():
                    column = litc[lamp, at(b), :]
                    for i in range(cols // LANES):
                        here = slice(i * LANES, (i + 1) * LANES)
                        model = (column * rates[lamp : lamp + 1, here]) * shape[:, here]
                        seen = frames[lamp, at(b), here].astype(F32)
                        done[lamp, at(b), here] = (seen - model).astype(BF16)
                    pltpu.make_async_copy(done.at[lamp, at(b)], out.at[lamp, at(b)], sem).start()

    pltpu.make_async_copy(frames, out, sem).wait()


def residual(flags, coef, rates, litc, ptab, frames):
    lamps, rows, cols = frames.shape
    vmem = pl.BlockSpec(memory_space=pltpu.VMEM)
    smem = pl.BlockSpec(memory_space=pltpu.SMEM)
    hbm = pl.BlockSpec(memory_space=pltpu.HBM)
    small = jax.ShapeDtypeStruct((MINE, K), F32)
    return pl.pallas_call(
        functools.partial(residual_kernel, lamps),
        out_shape=(small, small, jax.ShapeDtypeStruct(frames.shape, BF16)),
        in_specs=[smem, vmem, vmem, vmem, vmem, vmem],
        out_specs=(vmem, vmem, hbm),
        scratch_shapes=[
            pltpu.VMEM((LANES, cols), BF16),
            pltpu.VMEM((2 * LANES, cols), F32),
            pltpu.VMEM((BLOCK, cols), F32),
            pltpu.VMEM((lamps, rows, cols), BF16),
            pltpu.SemaphoreType.DMA,
        ],
        compiler_params=pltpu.CompilerParams(vmem_limit_bytes=24 << 20),
        name="residual",
    )(flags, coef, rates, litc, ptab, frames)


def body(frames, amplitude, line_start, bundle_width, fiber_bundle, trace_coef, width_coef):
    nrow = frames.shape[1] * lax.axis_size("rows")
    bundle = fiber_bundle.reshape(1, -1)
    coef, rates, litc, flags, ptab = fit(
        line_start, bundle_width, bundle, amplitude, trace_coef, width_coef, frames, nrow
    )
    return residual(flags, coef, rates, litc, ptab, frames)


def solution(mesh):
    placed = (
        P("fib", "rows", None),
        P("fib", None),
        P("fib", None),
        P(),
        P(),
        P(("rows", "fib"), None),
        P(("rows", "fib"), None),
    )
    return jax.shard_map(
        body,
        mesh=mesh,
        in_specs=placed,
        out_specs=(P(("rows", "fib"), None), P(("rows", "fib"), None), P("fib", "rows", None)),
        check_vma=False,
    )
```

```python
import functools
import itertools
import math

import jax
import jax.numpy as jnp
import numpy as np
from jax import lax
from jax.experimental import pallas as pl
from jax.experimental.pallas import tpu as pltpu
from jax.sharding import PartitionSpec as P

K = 11
PIX = 8
WIN = 8
ITERS = 3
LANES = 128
NDEV = 128
PLANES = 4
PER = 32
MINE = 4
SLOT = 32
KAPPA = math.sqrt(0.5 / math.log(2.0))
F32 = jnp.float32
BF16 = jnp.bfloat16
MESH = pl.DeviceIdType.MESH
HIGH = lax.Precision.HIGHEST


def adams_factor(order):
    value = 1.0
    for index in range(1, order + 1):
        value = value * (2.0 * index - 1.0) / index
    return value


def product_table():
    table = np.zeros((2 * K - 1, K, K))
    for a in range(K):
        for b in range(K):
            for m in range(min(a, b) + 1):
                target = a + b - 2 * m
                weight = adams_factor(m) * adams_factor(a - m) * adams_factor(b - m)
                weight = weight / adams_factor(a + b - m)
                weight = weight * (2.0 * target + 1.0) / (2.0 * (a + b - m) + 1.0)
                table[target, a, b] += weight
    return table


MOMENTS = 2 * K - 1
GRAD0 = 3 * MOMENTS
PACK = GRAD0 + 2 * K


def link_table():
    link = product_table()
    out = np.zeros((LANES, 24 * SLOT))
    for i in range(2 * K):
        for k in range(2 * K):
            which = (i >= K) + (k >= K)
            damp = 1.5 if i == k else 1.0
            out[which * MOMENTS : (which + 1) * MOMENTS, i * SLOT + k] = damp * link[:, i % K, k % K]
        out[GRAD0 + i, i * SLOT + 2 * K] = 1.0
    high = jnp.asarray(out, F32).astype(BF16)
    low = (jnp.asarray(out, F32) - high.astype(F32)).astype(BF16)
    return jnp.concatenate([high, low], axis=0)


def iota(shape, dim):
    return lax.broadcasted_iota(jnp.int32, shape, dim)


def legendre(t, count):
    polys = [jnp.ones_like(t), t]
    for n in range(1, count - 1):
        slope = t * ((2 * n + 1) / (n + 1))
        polys.append(slope * polys[n] - (n / (n + 1)) * polys[n - 1])
    return polys[:count]


def t_of(row, total):
    return (2.0 * row.astype(F32) + 1.0) / total - 1.0


def pick(x, lanes):
    return jnp.take_along_axis(x, lanes, axis=1)


def split(x):
    high = x.astype(BF16)
    return high, (x - high.astype(F32)).astype(BF16)


def lit_row(starts, lamp, lines, first):
    row = first + iota((1, LANES), 1)
    hit = jnp.zeros((1, LANES), F32)
    for i in range(lines):
        low = starts[lamp, i]
        hit = jnp.where((row >= low) & (row < low + WIN), 1.0, hit)
    return hit


def base_row(fiber_bundle, bundle_width, bundles):
    out = jnp.zeros(fiber_bundle.shape, F32)
    for b in range(bundles):
        out = jnp.where(fiber_bundle == b, bundle_width[b], out)
    return out


def offsets():
    every = itertools.product(range(PLANES), range(4), range(2), range(4))
    hops = lambda o: sum(min(o[i], 4 - o[i]) for i in (0, 1, 3))
    return sorted((o for o in every if any(o)), key=lambda o: (-hops(o), o[2]))


def fit_kernel(
    lamps, lines, bundles, nrow,
    starts_hbm, bundle_hbm, fiber_hbm, amp_hbm, trace_hbm, width_hbm, link_hbm, frames_hbm,
    out, rates, litc, flags, ptab,
    starts, bundle_width, fiber_bundle, amplitude, trace, width,
    frames, ft, fq, a2, invb, mix, px, tb, xq, w, link, row, ag, mom, rs,
    in_sem, small_sem, link_sem, ag_send, ag_recv, rs_send, rs_recv,
):
    my_row, my_fib = lax.axis_index("rows"), lax.axis_index("fib")
    me = my_row * 4 + my_fib
    my_z, my_y, my_core = my_row // 8, (my_row // 2) % 4, my_row % 2
    first = my_row * LANES
    zs = [(my_z + i) % PLANES for i in range(PLANES)]
    ys = [(my_y + i) % 4 for i in range(4)]
    cores = [my_core, 1 - my_core]
    fibs = [(my_fib + i) % 4 for i in range(4)]
    inner = {(y, c): ys[y] * 2 + cores[c] for y in range(4) for c in range(2)}
    rows_of = {(z, y, c): zs[z] * 8 + inner[y, c] for z in range(PLANES) for y, c in inner}

    barrier = pltpu.get_barrier_semaphore()
    for off in offsets():
        peer = (rows_of[off[:3]], fibs[off[3]])
        pl.semaphore_signal(barrier, inc=1, device_id=peer, device_id_type=MESH)

    small = [
        pltpu.make_async_copy(a, b, small_sem.at[i])
        for i, (a, b) in enumerate(
            (
                (trace_hbm, trace),
                (width_hbm, width),
                (starts_hbm, starts),
                (bundle_hbm, bundle_width),
                (fiber_hbm, fiber_bundle),
                (amp_hbm, amplitude),
            )
        )
    ]
    for copy in small:
        copy.start()
    for lamp in range(lamps):
        pltpu.make_async_copy(frames_hbm.at[lamp], frames.at[lamp], in_sem.at[lamp]).start()
    pltpu.make_async_copy(link_hbm, link, link_sem).start()

    def tell_everyone(step):
        for off in offsets():
            pltpu.make_async_remote_copy(
                src_ref=row.at[step],
                dst_ref=ag.at[step, me],
                send_sem=ag_send.at[step],
                recv_sem=ag_recv.at[step, my_z],
                device_id=(rows_of[off[:3]], fibs[off[3]]),
                device_id_type=MESH,
            ).start()
        pltpu.make_async_copy(row.at[step], ag.at[step, me], ag_recv.at[step, my_z]).start()

    for copy in small:
        copy.wait()

    row[0] = jnp.zeros((1, LANES), F32)
    for j in range(MINE):
        row[0, :, SLOT * j : SLOT * j + K] = trace[j : j + 1, :]
        row[0, :, SLOT * j + K : SLOT * j + 2 * K] = width[j : j + 1, :]

    px[...] = jnp.zeros(px.shape, BF16)
    sub = iota((SLOT, LANES), 0)
    polys = legendre(t_of(first + iota((1, LANES), 1), nrow), K)
    for part in range(2):
        table = jnp.zeros((SLOT, LANES), F32)
        for k in range(K):
            table = jnp.where(sub == k + part * K, (1.0, -1.0)[part] * polys[k], table)
        high, low = split(table)
        for j in range(MINE):
            lanes = pl.ds((2 * j + part) * LANES, LANES)
            px[pl.ds(SLOT * j, SLOT), lanes] = high
            px[pl.ds(LANES + SLOT * j, SLOT), lanes] = low

    lane = iota((LANES, LANES), 1)
    degree = jnp.where(lane < GRAD0, lane % MOMENTS, (lane - GRAD0) % K)
    degree = jnp.where(lane < GRAD0 + 2 * K, degree, -1)
    wide = legendre(t_of(first + iota((LANES, LANES), 0), nrow), MOMENTS)
    table = jnp.zeros((LANES, LANES), F32)
    for k in range(MOMENTS):
        table = jnp.where(degree == k, wide[k], table)
    table = table * jnp.where(lane < GRAD0, KAPPA**-4, KAPPA**-2)
    ends = [0, MOMENTS, 2 * MOMENTS, GRAD0, GRAD0 + K, GRAD0 + 2 * K]
    for a in range(5):
        inside = (lane >= ends[a]) & (lane < ends[a + 1])
        high, low = split(jnp.where(inside, table, 0.0))
        for at in (2 * a, 2 * a + 1):
            tb[at * LANES : (at + 1) * LANES, 0:LANES] = high
            tb[at * LANES : (at + 1) * LANES, LANES : 2 * LANES] = low

    pl.semaphore_wait(barrier, NDEV - 1)
    tell_everyone(0)

    def for_residual():
        lane = iota((LANES, LANES), 1)
        polys = legendre(t_of(first + iota((LANES, LANES), 0), nrow), K)
        for part in range(2):
            table = jnp.zeros((LANES, LANES), F32)
            for k in range(K):
                table = jnp.where(lane % SLOT == k + part * K, (1.0, -1.0)[part] * polys[k], table)
            high = table.astype(BF16).astype(F32)
            table = jnp.where(lane < 2 * SLOT, high, jnp.where(lane < 3 * SLOT, table - high, 0.0))
            ptab[part * LANES : (part + 1) * LANES, :] = table.astype(BF16)
        base = base_row(fiber_bundle[...], bundle_width, bundles)
        rate = jnp.broadcast_to(KAPPA / base, (8, amplitude.shape[1]))
        for lamp in range(lamps):
            rate = jnp.where(iota(rate.shape, 0) == lamp, amplitude[lamp : lamp + 1, :], rate)
        spread = iota((8, LANES), 1) // PIX
        for b in range(32):
            part = lax.slice_in_dim(rate, (b // 8) * LANES, (b // 8 + 1) * LANES, axis=1)
            rates[:, b * LANES : (b + 1) * LANES] = jnp.take_along_axis(
                part, spread + 16 * (b % 8), axis=1
            )

    lits = [lit_row(starts, lamp, lines, first) for lamp in range(lamps)]
    for lamp in range(lamps):
        litc[lamp] = jnp.transpose(jnp.broadcast_to(lits[lamp], (LANES, LANES)))
    base = base_row(fiber_bundle[...], bundle_width, bundles)
    sub8 = iota((8, LANES), 0)
    sub8w = iota((8, amplitude.shape[1]), 0)
    amp = jnp.zeros(sub8w.shape, F32)
    lit8 = jnp.zeros((8, LANES), F32)
    for lamp in range(lamps):
        amp = jnp.where(sub8w == lamp, amplitude[lamp : lamp + 1, :], amp)
        lit8 = jnp.where(sub8 == lamp, lits[lamp], lit8)
    blocks = (iota((LANES, LANES), 0) // 16 == iota((LANES, LANES), 1)).astype(F32)
    flags[...] = jnp.dot(lit8, blocks, preferred_element_type=F32).astype(jnp.int32)
    left = jnp.where(sub8w == lamps, KAPPA / base, amp * amp)
    right = jnp.concatenate([lit8, jnp.where(sub8 == lamps, 1.0, jnp.zeros((8, LANES), F32))], axis=1)
    mixed = lax.dot_general(
        jnp.transpose(left), right, (((1,), (0,)), ((), ())), precision=HIGH, preferred_element_type=F32
    )
    for part, dest in enumerate((a2, invb)):
        mix[...] = mixed[:, part * LANES : (part + 1) * LANES]
        for j in range(MINE):
            dest[j] = mix[pl.ds(j, NDEV, stride=MINE), :]

    for lamp in range(lamps):
        pltpu.make_async_copy(frames_hbm.at[lamp], frames.at[lamp], in_sem.at[lamp]).wait()
    spread = iota((8, LANES), 1) // PIX
    for b in range(32):
        cols = pl.ds(b * LANES, LANES)
        part = lax.slice_in_dim(amp, (b // 8) * LANES, (b // 8 + 1) * LANES, axis=1)
        bright = jnp.take_along_axis(part, spread + 16 * (b % 8), axis=1)
        total = jnp.zeros((LANES, LANES), F32)
        for lamp in range(lamps):
            weight = litc[lamp] * bright[lamp : lamp + 1, :]
            total = total + weight * frames[lamp, :, cols].astype(F32)
        ft[pl.ds(b * LANES, LANES), :] = jnp.transpose(total)

    @pl.loop(0, 32)
    def _(q):
        fq[q] = ft[pl.ds(q, NDEV, stride=32), :]

    for_residual()
    pltpu.make_async_copy(link_hbm, link, link_sem).wait()

    def profiles(step, hops, slot):
        starts_at = [pl.multiple_of(zs[hop] * PER, PER) for hop in hops]
        for hop, d0 in zip(hops, starts_at):
            here = ag.at[step, pl.ds(d0, PER)]
            pltpu.make_async_copy(here, here, ag_recv.at[step, zs[hop]]).wait()
        coef = jnp.concatenate([ag[step, pl.ds(d0, PER), 0, :] for d0 in starts_at], axis=0)
        high, low = split(coef)
        lhs = jnp.concatenate(
            [jnp.concatenate([high, high], axis=1), jnp.concatenate([low, low], axis=1)], axis=0
        )
        both = jnp.dot(lhs, px[...], preferred_element_type=F32)
        xq[slot] = both[0 : 2 * PER] + both[2 * PER : 4 * PER]

    def column_sums(hops, slot):
        starts_at = [pl.multiple_of(zs[hop] * PER, PER) for hop in hops]
        for j in range(MINE):
            for part in range(4):
                rows = slice(part * 16, part * 16 + 16)
                d0 = starts_at[part // 2]
                drows = pl.ds(pl.multiple_of(d0 + (part % 2) * 16, 16), 16)
                x = xq[slot, rows, (2 * j) * LANES : (2 * j + 1) * LANES]
                inv = jnp.exp(xq[slot, rows, (2 * j + 1) * LANES : (2 * j + 2) * LANES]) * invb[j, drows, :]
                bright2 = a2[j, drows, :]
                sxx = sxs = sss = hx = hs = jnp.zeros((16, LANES), F32)
                u = (-(PIX - 1) / 2.0 - x) * inv
                for p in range(PIX):
                    g = jnp.exp2(-(u * u))
                    gu = g * u
                    m = gu * gu
                    n = m * u
                    tg = (fq[PIX * j + p, drows, :] - bright2 * g) * gu
                    sxx = sxx + m
                    sxs = sxs + n
                    sss = sss + n * u
                    hx = hx + tg
                    hs = hs + tg * u
                    u = u + inv
                sums = (bright2 * sxx * inv * inv, bright2 * sxs * inv, bright2 * sss, inv * hx, hs)
                wrows = slice(j * 2 * PER + part * 16, j * 2 * PER + part * 16 + 16)
                for a in range(5):
                    h, l = split(sums[a])
                    w[slot, wrows, 2 * a * LANES : (2 * a + 1) * LANES] = h
                    w[slot, wrows, (2 * a + 1) * LANES : (2 * a + 2) * LANES] = l

    def moments_of(slot):
        both = jnp.dot(w[slot], tb[...], preferred_element_type=F32)
        return both[:, 0:LANES] + both[:, LANES : 2 * LANES]

    def send(step, hops, moments):
        starts_at = [pl.multiple_of(zs[hop] * PER, PER) for hop in hops]
        lane = iota((PER, LANES), 1)
        for i, (hop, d0) in enumerate(zip(hops, starts_at)):
            at = [moments[(2 * j + i) * PER : (2 * j + i + 1) * PER, :] for j in range(MINE)]
            second = pltpu.roll(at[1], PACK, axis=1)
            third = pltpu.roll(at[2], LANES - PACK, axis=1)
            drows = pl.ds(d0, PER)
            mom[step, drows, 0, :] = jnp.where(lane < PACK, at[0], second)
            mom[step, drows, 1, :] = jnp.where(lane < 2 * PACK - LANES, second, third)
            mom[step, drows, 2, :] = at[3]
            for off in offsets():
                if off[0] == hop:
                    peer = (rows_of[off[:3]], fibs[off[3]])
                    pltpu.make_async_remote_copy(
                        src_ref=mom.at[step, peer[0] * 4 + peer[1]],
                        dst_ref=rs.at[step, me],
                        send_sem=rs_send.at[step],
                        recv_sem=rs_recv.at[step, my_z],
                        device_id=peer,
                        device_id_type=MESH,
                    ).start()
            if hop == 0:
                mine = rs.at[step, me]
                pltpu.make_async_copy(mom.at[step, me], mine, rs_recv.at[step, my_z]).start()

    def solve(step):
        total = jnp.zeros((3, LANES), F32)
        for hop in (2, 1, 3, 0):
            d0 = pl.multiple_of(zs[hop] * PER, PER)
            here = rs.at[step, pl.ds(d0, PER)]
            pltpu.make_async_copy(here, here, rs_recv.at[step, zs[hop]]).wait()
            parts = [rs[step, pl.ds(d0 + 8 * i, 8)].sum(axis=0) for i in range(4)]
            total = total + ((parts[0] + parts[1]) + (parts[2] + parts[3]))
        lane = iota((1, LANES), 1)
        top, middle, bottom = total[0:1], total[1:2], total[2:3]
        second = pltpu.roll(jnp.where(lane < PACK, middle, top), LANES - PACK, axis=1)
        third = pltpu.roll(middle, PACK, axis=1)
        sub = iota((MINE, LANES), 0)
        total = jnp.where(
            sub < 2, jnp.where(sub == 0, top, second), jnp.where(sub == 2, third, bottom)
        )
        high = total.astype(BF16).astype(F32)
        both = jnp.concatenate([high, total - high], axis=0)
        lhs = jnp.concatenate([both, both], axis=1).astype(BF16)
        both = jnp.dot(lhs, link[...], preferred_element_type=F32)
        both = both[0:MINE] + both[MINE : 2 * MINE]
        lane = iota((MINE, LANES), 1)
        group, within = lane // SLOT, lane % SLOT
        system = []
        for v in range(6):
            block = both[:, v * LANES : (v + 1) * LANES]
            system.append(jnp.where(within == 4 * v + group, block + 1.0, block))
        for v in range(6):
            width_of = min(4, 2 * K - 4 * v)
            mine = range(width_of)
            ahead = [pick(system[v], within + SLOT * g) for g in mine]
            pivot = [
                [pick(system[v], jnp.full_like(lane, SLOT * g + 4 * v + b)) for b in mine] for g in mine
            ]
            cols = [[pick(x, group * SLOT + 4 * v + b) for b in mine] for x in system]
            for g in mine:
                unit = 1.0 / pivot[g][g]
                ahead[g] = ahead[g] * unit
                for b in range(g + 1, width_of):
                    pivot[g][b] = pivot[g][b] * unit
                for c in mine:
                    if c != g:
                        ahead[c] = ahead[c] - pivot[c][g] * ahead[g]
                        for b in range(g + 1, width_of):
                            pivot[c][b] = pivot[c][b] - pivot[c][g] * pivot[g][b]
            for u in range(6):
                taken = cols[u][0] * ahead[0]
                for b in range(1, width_of):
                    taken = taken + cols[u][b] * ahead[b]
                system[u] = system[u] - taken
                if u == v:
                    for g in mine:
                        system[u] = jnp.where(group == g, ahead[g], system[u])
        found = jnp.zeros((MINE, LANES), F32)
        for v in range(6):
            got = pick(system[v], (within % 4) * SLOT + 2 * K)
            found = jnp.where((within // 4 == v) & (within < 2 * K), got, found)
        found = jnp.where(iota((MINE, LANES), 0) == group, found, 0.0)
        row[step + 1] = row[step] + found.sum(axis=0, keepdims=True)

    @pl.loop(0, ITERS)
    def _(step):
        early, late = (2, 1), (3, 0)
        profiles(step, early, 0)
        profiles(step, late, 1)
        column_sums(early, 0)
        moments = moments_of(0)
        column_sums(late, 1)
        send(step, early, moments)
        send(step, late, moments_of(1))
        solve(step)
        tell_everyone(step + 1)
        sent = mom.at[step, pl.ds(0, NDEV - 1)]
        pltpu.make_async_copy(sent, sent, rs_send.at[step]).wait()
        told = ag.at[step, pl.ds(0, NDEV - 1)]
        pltpu.make_async_copy(told, told, ag_send.at[step]).wait()

    for z in range(PLANES):
        here = ag.at[ITERS, pl.ds(z * PER, PER)]
        pltpu.make_async_copy(here, here, ag_recv.at[ITERS, z]).wait()
    out[...] = ag[ITERS, :, 0, :]
    told = ag.at[ITERS, pl.ds(0, NDEV - 1)]
    pltpu.make_async_copy(told, told, ag_send.at[ITERS]).wait()


def fit(starts, bundle_width, fiber_bundle, amplitude, trace, width, frames, nrow):
    lamps, rows, cols = frames.shape
    vmem = pl.BlockSpec(memory_space=pltpu.VMEM)
    hbm = pl.BlockSpec(memory_space=pltpu.HBM)
    dma = pltpu.SemaphoreType.DMA
    like = lambda space, x: space(x.shape, x.dtype)
    kernel = functools.partial(fit_kernel, lamps, starts.shape[1], bundle_width.shape[0], nrow)
    shape = jax.ShapeDtypeStruct
    return pl.pallas_call(
        kernel,
        out_shape=(
            shape((NDEV, LANES), F32),
            shape((8, cols), F32),
            shape((lamps, LANES, LANES), F32),
            shape((8, LANES), jnp.int32),
            shape((2 * LANES, LANES), BF16),
        ),
        in_specs=[hbm] * 8,
        out_specs=(vmem,) * 5,
        scratch_shapes=[
            like(pltpu.SMEM, starts),
            like(pltpu.SMEM, bundle_width),
            like(pltpu.VMEM, fiber_bundle),
            like(pltpu.VMEM, amplitude),
            like(pltpu.VMEM, trace),
            like(pltpu.VMEM, width),
            pltpu.VMEM((lamps, rows, cols), BF16),
            pltpu.VMEM((cols, LANES), F32),
            pltpu.VMEM((32, NDEV, LANES), F32),
            pltpu.VMEM((MINE, NDEV, LANES), F32),
            pltpu.VMEM((MINE, NDEV, LANES), F32),
            pltpu.VMEM((MINE * NDEV, LANES), F32),
            pltpu.VMEM((2 * LANES, 8 * LANES), BF16),
            pltpu.VMEM((10 * LANES, 2 * LANES), BF16),
            pltpu.VMEM((2, 2 * PER, 8 * LANES), F32),
            pltpu.VMEM((2, 2 * LANES, 10 * LANES), BF16),
            pltpu.VMEM((2 * LANES, 24 * SLOT), BF16),
            pltpu.VMEM((ITERS + 1, 1, LANES), F32),
            pltpu.VMEM((ITERS + 1, NDEV, 1, LANES), F32),
            pltpu.VMEM((ITERS, NDEV, 3, LANES), F32),
            pltpu.VMEM((ITERS, NDEV, 3, LANES), F32),
            dma((lamps,)),
            dma((6,)),
            dma,
            dma((ITERS + 1,)),
            dma((ITERS + 1, PLANES)),
            dma((ITERS,)),
            dma((ITERS, PLANES)),
        ],
        compiler_params=pltpu.CompilerParams(
            collective_id=0, has_side_effects=True, vmem_limit_bytes=24 << 20
        ),
        name="fit",
    )(
        *(
            pltpu.with_memory_space_constraint(x, pltpu.HBM)
            for x in (starts, bundle_width, fiber_bundle, amplitude, trace, width, link_table(), frames)
        )
    )


BLOCK = 16


def residual_kernel(
    lamps,
    flags, coef, rates, litc, ptab, frames,
    trace_out, width_out, out,
    table, xq, shape, done, sem,
):
    me = lax.axis_index("rows") * 4 + lax.axis_index("fib")
    blocks = frames.shape[1] // BLOCK
    cols = frames.shape[2]

    def at(b):
        return pl.ds(pl.multiple_of(b * BLOCK, BLOCK), BLOCK)

    @pl.loop(0, blocks)
    def _(b):
        for lamp in range(lamps):

            @pl.when(flags[lamp, b] == 0)
            def _():
                pltpu.make_async_copy(frames.at[lamp, at(b)], out.at[lamp, at(b)], sem).start()

    mine = coef[pl.ds(me, 1), :]
    for j in range(MINE):
        trace_out[j : j + 1, :] = mine[:, SLOT * j : SLOT * j + K]
        width_out[j : j + 1, :] = mine[:, SLOT * j + K : SLOT * j + 2 * K]

    turned = jnp.transpose(coef[...])
    lane = iota((SLOT, LANES), 1)
    table[3 * SLOT : 4 * SLOT, :] = jnp.zeros((SLOT, cols), BF16)
    for fb in range(4):
        pick = 32 * fb + lane // MINE
        named = jnp.zeros((SLOT, LANES), F32)
        for j in range(MINE):
            got = jnp.take_along_axis(turned[SLOT * j : SLOT * (j + 1), :], pick, axis=1)
            named = jnp.where(lane % MINE == j, got, named)
        for b in range(8):
            here = pl.ds((8 * fb + b) * LANES, LANES)
            got = jnp.take_along_axis(named, lane // PIX + 16 * b, axis=1)
            high, low = split(got)
            table[0:SLOT, here] = high
            table[SLOT : 2 * SLOT, here] = low
            table[2 * SLOT : 3 * SLOT, here] = high
    xq[...] = jnp.dot(ptab[...], table[...], preferred_element_type=F32)

    offset = (iota((1, LANES), 1) % PIX).astype(F32) - (PIX - 1) / 2.0

    @pl.loop(0, blocks)
    def _(b):
        lit = flags[0, b]
        for lamp in range(1, lamps):
            lit = lit + flags[lamp, b]

        @pl.when(lit > 0)
        def _():
            for i in range(cols // LANES):
                here = slice(i * LANES, (i + 1) * LANES)
                x = xq[at(b), here]
                q = xq[pl.ds(pl.multiple_of(LANES + b * BLOCK, BLOCK), BLOCK), here]
                u = (offset - x) * (jnp.exp(q) * rates[lamps : lamps + 1, here])
                shape[:, here] = jnp.exp2(-(u * u))
            for lamp in range(lamps):

                @pl.when(flags[lamp, b] > 0)
                def _():
                    column = litc[lamp, at(b), :]
                    for i in range(cols // LANES):
                        here = slice(i * LANES, (i + 1) * LANES)
                        model = (column * rates[lamp : lamp + 1, here]) * shape[:, here]
                        seen = frames[lamp, at(b), here].astype(F32)
                        done[lamp, at(b), here] = (seen - model).astype(BF16)
                    pltpu.make_async_copy(done.at[lamp, at(b)], out.at[lamp, at(b)], sem).start()

    pltpu.make_async_copy(frames, out, sem).wait()


def residual(flags, coef, rates, litc, ptab, frames):
    lamps, rows, cols = frames.shape
    vmem = pl.BlockSpec(memory_space=pltpu.VMEM)
    smem = pl.BlockSpec(memory_space=pltpu.SMEM)
    hbm = pl.BlockSpec(memory_space=pltpu.HBM)
    small = jax.ShapeDtypeStruct((MINE, K), F32)
    return pl.pallas_call(
        functools.partial(residual_kernel, lamps),
        out_shape=(small, small, jax.ShapeDtypeStruct(frames.shape, BF16)),
        in_specs=[smem, vmem, vmem, vmem, vmem, vmem],
        out_specs=(vmem, vmem, hbm),
        scratch_shapes=[
            pltpu.VMEM((LANES, cols), BF16),
            pltpu.VMEM((2 * LANES, cols), F32),
            pltpu.VMEM((BLOCK, cols), F32),
            pltpu.VMEM((lamps, rows, cols), BF16),
            pltpu.SemaphoreType.DMA,
        ],
        compiler_params=pltpu.CompilerParams(vmem_limit_bytes=24 << 20),
        name="residual",
    )(flags, coef, rates, litc, ptab, frames)


def body(frames, amplitude, line_start, bundle_width, fiber_bundle, trace_coef, width_coef):
    nrow = frames.shape[1] * lax.axis_size("rows")
    bundle = fiber_bundle.reshape(1, -1)
    coef, rates, litc, flags, ptab = fit(
        line_start, bundle_width, bundle, amplitude, trace_coef, width_coef, frames, nrow
    )
    return residual(flags, coef, rates, litc, ptab, frames)


def solution(mesh):
    placed = (
        P("fib", "rows", None),
        P("fib", None),
        P("fib", None),
        P(),
        P(),
        P(("rows", "fib"), None),
        P(("rows", "fib"), None),
    )
    return jax.shard_map(
        body,
        mesh=mesh,
        in_specs=placed,
        out_specs=(P(("rows", "fib"), None), P(("rows", "fib"), None), P("fib", "rows", None)),
        check_vma=False,
    )
```

```python
import functools
import itertools
import math

import jax
import jax.numpy as jnp
import numpy as np
from jax import lax
from jax.experimental import pallas as pl
from jax.experimental.pallas import tpu as pltpu
from jax.sharding import PartitionSpec as P

K = 11
PIX = 8
WIN = 8
ITERS = 3
LANES = 128
NDEV = 128
PLANES = 4
PER = 32
MINE = 4
SLOT = 32
KAPPA = math.sqrt(0.5)
F32 = jnp.float32
BF16 = jnp.bfloat16
MESH = pl.DeviceIdType.MESH
HIGH = lax.Precision.HIGHEST


def adams_factor(order):
    value = 1.0
    for index in range(1, order + 1):
        value = value * (2.0 * index - 1.0) / index
    return value


def product_table():
    table = np.zeros((2 * K - 1, K, K))
    for a in range(K):
        for b in range(K):
            for m in range(min(a, b) + 1):
                target = a + b - 2 * m
                weight = adams_factor(m) * adams_factor(a - m) * adams_factor(b - m)
                weight = weight / adams_factor(a + b - m)
                weight = weight * (2.0 * target + 1.0) / (2.0 * (a + b - m) + 1.0)
                table[target, a, b] += weight
    return table


MOMENTS = 2 * K - 1
GRAD0 = 3 * MOMENTS
PACK = GRAD0 + 2 * K


def link_table():
    link = product_table()
    out = np.zeros((LANES, 24 * SLOT))
    for i in range(2 * K):
        for k in range(2 * K):
            which = (i >= K) + (k >= K)
            damp = 1.5 if i == k else 1.0
            out[which * MOMENTS : (which + 1) * MOMENTS, i * SLOT + k] = damp * link[:, i % K, k % K]
        out[GRAD0 + i, i * SLOT + 2 * K] = 1.0
    high = jnp.asarray(out, F32).astype(BF16)
    low = (jnp.asarray(out, F32) - high.astype(F32)).astype(BF16)
    return jnp.concatenate([high, low], axis=0)


def iota(shape, dim):
    return lax.broadcasted_iota(jnp.int32, shape, dim)


def legendre(t, count):
    polys = [jnp.ones_like(t), t]
    for n in range(1, count - 1):
        slope = t * ((2 * n + 1) / (n + 1))
        polys.append(slope * polys[n] - (n / (n + 1)) * polys[n - 1])
    return polys[:count]


def t_of(row, total):
    return (2.0 * row.astype(F32) + 1.0) / total - 1.0


def pick(x, lanes):
    return jnp.take_along_axis(x, lanes, axis=1)


def split(x):
    high = x.astype(BF16)
    return high, (x - high.astype(F32)).astype(BF16)


def lit_row(starts, lamp, lines, first):
    row = first + iota((1, LANES), 1)
    hit = jnp.zeros((1, LANES), F32)
    for i in range(lines):
        low = starts[lamp, i]
        hit = jnp.where((row >= low) & (row < low + WIN), 1.0, hit)
    return hit


def base_row(fiber_bundle, bundle_width, bundles):
    out = jnp.zeros(fiber_bundle.shape, F32)
    for b in range(bundles):
        out = jnp.where(fiber_bundle == b, bundle_width[b], out)
    return out


def offsets():
    every = itertools.product(range(PLANES), range(4), range(2), range(4))
    hops = lambda o: sum(min(o[i], 4 - o[i]) for i in (0, 1, 3))
    return sorted((o for o in every if any(o)), key=lambda o: (-hops(o), o[2]))


def fit_kernel(
    lamps, lines, bundles, nrow,
    starts_hbm, bundle_hbm, fiber_hbm, amp_hbm, trace_hbm, width_hbm, link_hbm, frames_hbm,
    out, rates, litc, flags, ptab,
    starts, bundle_width, fiber_bundle, amplitude, trace, width,
    frames, ft, fq, a2, invb, mix, px, tb, xq, w, link, row, ag, mom, rs,
    in_sem, small_sem, link_sem, ag_send, ag_recv, rs_send, rs_recv,
):
    my_row, my_fib = lax.axis_index("rows"), lax.axis_index("fib")
    me = my_row * 4 + my_fib
    my_z, my_y, my_core = my_row // 8, (my_row // 2) % 4, my_row % 2
    first = my_row * LANES
    zs = [(my_z + i) % PLANES for i in range(PLANES)]
    ys = [(my_y + i) % 4 for i in range(4)]
    cores = [my_core, 1 - my_core]
    fibs = [(my_fib + i) % 4 for i in range(4)]
    inner = {(y, c): ys[y] * 2 + cores[c] for y in range(4) for c in range(2)}
    rows_of = {(z, y, c): zs[z] * 8 + inner[y, c] for z in range(PLANES) for y, c in inner}

    barrier = pltpu.get_barrier_semaphore()
    for off in offsets():
        peer = (rows_of[off[:3]], fibs[off[3]])
        pl.semaphore_signal(barrier, inc=1, device_id=peer, device_id_type=MESH)

    small = [
        pltpu.make_async_copy(a, b, small_sem.at[i])
        for i, (a, b) in enumerate(
            (
                (trace_hbm, trace),
                (width_hbm, width),
                (starts_hbm, starts),
                (bundle_hbm, bundle_width),
                (fiber_hbm, fiber_bundle),
                (amp_hbm, amplitude),
            )
        )
    ]
    for copy in small:
        copy.start()
    for lamp in range(lamps):
        pltpu.make_async_copy(frames_hbm.at[lamp], frames.at[lamp], in_sem.at[lamp]).start()
    pltpu.make_async_copy(link_hbm, link, link_sem).start()

    def tell_everyone(step):
        for off in offsets():
            pltpu.make_async_remote_copy(
                src_ref=row.at[step],
                dst_ref=ag.at[step, me],
                send_sem=ag_send.at[step],
                recv_sem=ag_recv.at[step, my_z],
                device_id=(rows_of[off[:3]], fibs[off[3]]),
                device_id_type=MESH,
            ).start()
        pltpu.make_async_copy(row.at[step], ag.at[step, me], ag_recv.at[step, my_z]).start()

    for copy in small:
        copy.wait()

    row[0] = jnp.zeros((1, LANES), F32)
    for j in range(MINE):
        row[0, :, SLOT * j : SLOT * j + K] = trace[j : j + 1, :]
        row[0, :, SLOT * j + K : SLOT * j + 2 * K] = width[j : j + 1, :]

    px[...] = jnp.zeros(px.shape, BF16)
    sub = iota((SLOT, LANES), 0)
    polys = legendre(t_of(first + iota((1, LANES), 1), nrow), K)
    for part in range(2):
        table = jnp.zeros((SLOT, LANES), F32)
        for k in range(K):
            table = jnp.where(sub == k + part * K, (1.0, -1.0)[part] * polys[k], table)
        high, low = split(table)
        for j in range(MINE):
            lanes = pl.ds((2 * j + part) * LANES, LANES)
            px[pl.ds(SLOT * j, SLOT), lanes] = high
            px[pl.ds(LANES + SLOT * j, SLOT), lanes] = low

    lane = iota((LANES, LANES), 1)
    degree = jnp.where(lane < GRAD0, lane % MOMENTS, (lane - GRAD0) % K)
    degree = jnp.where(lane < GRAD0 + 2 * K, degree, -1)
    wide = legendre(t_of(first + iota((LANES, LANES), 0), nrow), MOMENTS)
    table = jnp.zeros((LANES, LANES), F32)
    for k in range(MOMENTS):
        table = jnp.where(degree == k, wide[k], table)
    table = table * jnp.where(lane < GRAD0, KAPPA**-4, KAPPA**-2)
    ends = [0, MOMENTS, 2 * MOMENTS, GRAD0, GRAD0 + K, GRAD0 + 2 * K]
    for a in range(5):
        inside = (lane >= ends[a]) & (lane < ends[a + 1])
        high, low = split(jnp.where(inside, table, 0.0))
        for at in (2 * a, 2 * a + 1):
            tb[at * LANES : (at + 1) * LANES, 0:LANES] = high
            tb[at * LANES : (at + 1) * LANES, LANES : 2 * LANES] = low

    pl.semaphore_wait(barrier, NDEV - 1)
    tell_everyone(0)

    def for_residual():
        lane = iota((LANES, LANES), 1)
        polys = legendre(t_of(first + iota((LANES, LANES), 0), nrow), K)
        for part in range(2):
            table = jnp.zeros((LANES, LANES), F32)
            for k in range(K):
                table = jnp.where(lane % SLOT == k + part * K, (1.0, -1.0)[part] * polys[k], table)
            high = table.astype(BF16).astype(F32)
            table = jnp.where(lane < 2 * SLOT, high, jnp.where(lane < 3 * SLOT, table - high, 0.0))
            ptab[part * LANES : (part + 1) * LANES, :] = table.astype(BF16)
        base = base_row(fiber_bundle[...], bundle_width, bundles)
        rate = jnp.broadcast_to(KAPPA / base, (8, amplitude.shape[1]))
        for lamp in range(lamps):
            rate = jnp.where(iota(rate.shape, 0) == lamp, amplitude[lamp : lamp + 1, :], rate)
        spread = iota((8, LANES), 1) // PIX
        for b in range(32):
            part = lax.slice_in_dim(rate, (b // 8) * LANES, (b // 8 + 1) * LANES, axis=1)
            rates[:, b * LANES : (b + 1) * LANES] = jnp.take_along_axis(
                part, spread + 16 * (b % 8), axis=1
            )

    lits = [lit_row(starts, lamp, lines, first) for lamp in range(lamps)]
    for lamp in range(lamps):
        litc[lamp] = jnp.transpose(jnp.broadcast_to(lits[lamp], (LANES, LANES)))
    base = base_row(fiber_bundle[...], bundle_width, bundles)
    sub8 = iota((8, LANES), 0)
    sub8w = iota((8, amplitude.shape[1]), 0)
    amp = jnp.zeros(sub8w.shape, F32)
    lit8 = jnp.zeros((8, LANES), F32)
    for lamp in range(lamps):
        amp = jnp.where(sub8w == lamp, amplitude[lamp : lamp + 1, :], amp)
        lit8 = jnp.where(sub8 == lamp, lits[lamp], lit8)
    blocks = (iota((LANES, LANES), 0) // 16 == iota((LANES, LANES), 1)).astype(F32)
    flags[...] = jnp.dot(lit8, blocks, preferred_element_type=F32).astype(jnp.int32)
    left = jnp.where(sub8w == lamps, KAPPA / base, amp * amp)
    right = jnp.concatenate([lit8, jnp.where(sub8 == lamps, 1.0, jnp.zeros((8, LANES), F32))], axis=1)
    mixed = lax.dot_general(
        jnp.transpose(left), right, (((1,), (0,)), ((), ())), precision=HIGH, preferred_element_type=F32
    )
    for part, dest in enumerate((a2, invb)):
        mix[...] = mixed[:, part * LANES : (part + 1) * LANES]
        for j in range(MINE):
            dest[j] = mix[pl.ds(j, NDEV, stride=MINE), :]

    for lamp in range(lamps):
        pltpu.make_async_copy(frames_hbm.at[lamp], frames.at[lamp], in_sem.at[lamp]).wait()
    spread = iota((8, LANES), 1) // PIX
    for b in range(32):
        cols = pl.ds(b * LANES, LANES)
        part = lax.slice_in_dim(amp, (b // 8) * LANES, (b // 8 + 1) * LANES, axis=1)
        bright = jnp.take_along_axis(part, spread + 16 * (b % 8), axis=1)
        total = jnp.zeros((LANES, LANES), F32)
        for lamp in range(lamps):
            weight = litc[lamp] * bright[lamp : lamp + 1, :]
            total = total + weight * frames[lamp, :, cols].astype(F32)
        ft[pl.ds(b * LANES, LANES), :] = jnp.transpose(total)

    @pl.loop(0, 32)
    def _(q):
        fq[q] = ft[pl.ds(q, NDEV, stride=32), :]

    for_residual()
    pltpu.make_async_copy(link_hbm, link, link_sem).wait()

    def profiles(step, hops, slot):
        starts_at = [pl.multiple_of(zs[hop] * PER, PER) for hop in hops]
        for hop, d0 in zip(hops, starts_at):
            here = ag.at[step, pl.ds(d0, PER)]
            pltpu.make_async_copy(here, here, ag_recv.at[step, zs[hop]]).wait()
        coef = jnp.concatenate([ag[step, pl.ds(d0, PER), 0, :] for d0 in starts_at], axis=0)
        high, low = split(coef)
        lhs = jnp.concatenate(
            [jnp.concatenate([high, high], axis=1), jnp.concatenate([low, low], axis=1)], axis=0
        )
        both = jnp.dot(lhs, px[...], preferred_element_type=F32)
        xq[slot] = both[0 : 2 * PER] + both[2 * PER : 4 * PER]

    def column_sums(hops, slot):
        starts_at = [pl.multiple_of(zs[hop] * PER, PER) for hop in hops]
        for j in range(MINE):
            for part in range(4):
                rows = slice(part * 16, part * 16 + 16)
                d0 = starts_at[part // 2]
                drows = pl.ds(pl.multiple_of(d0 + (part % 2) * 16, 16), 16)
                x = xq[slot, rows, (2 * j) * LANES : (2 * j + 1) * LANES]
                inv = jnp.exp(xq[slot, rows, (2 * j + 1) * LANES : (2 * j + 2) * LANES]) * invb[j, drows, :]
                bright2 = a2[j, drows, :]
                sxx = sxs = sss = hx = hs = jnp.zeros((16, LANES), F32)
                u = (-(PIX - 1) / 2.0 - x) * inv
                for p in range(PIX):
                    g = jnp.exp(-(u * u))
                    gu = g * u
                    m = gu * gu
                    n = m * u
                    tg = (fq[PIX * j + p, drows, :] - bright2 * g) * gu
                    sxx = sxx + m
                    sxs = sxs + n
                    sss = sss + n * u
                    hx = hx + tg
                    hs = hs + tg * u
                    u = u + inv
                sums = (bright2 * sxx * inv * inv, bright2 * sxs * inv, bright2 * sss, inv * hx, hs)
                wrows = slice(j * 2 * PER + part * 16, j * 2 * PER + part * 16 + 16)
                for a in range(5):
                    h, l = split(sums[a])
                    w[slot, wrows, 2 * a * LANES : (2 * a + 1) * LANES] = h
                    w[slot, wrows, (2 * a + 1) * LANES : (2 * a + 2) * LANES] = l

    def moments_of(slot):
        both = jnp.dot(w[slot], tb[...], preferred_element_type=F32)
        return both[:, 0:LANES] + both[:, LANES : 2 * LANES]

    def send(step, hops, moments):
        starts_at = [pl.multiple_of(zs[hop] * PER, PER) for hop in hops]
        lane = iota((PER, LANES), 1)
        for i, (hop, d0) in enumerate(zip(hops, starts_at)):
            at = [moments[(2 * j + i) * PER : (2 * j + i + 1) * PER, :] for j in range(MINE)]
            second = pltpu.roll(at[1], PACK, axis=1)
            third = pltpu.roll(at[2], LANES - PACK, axis=1)
            drows = pl.ds(d0, PER)
            mom[step, drows, 0, :] = jnp.where(lane < PACK, at[0], second)
            mom[step, drows, 1, :] = jnp.where(lane < 2 * PACK - LANES, second, third)
            mom[step, drows, 2, :] = at[3]
            for off in offsets():
                if off[0] == hop:
                    peer = (rows_of[off[:3]], fibs[off[3]])
                    pltpu.make_async_remote_copy(
                        src_ref=mom.at[step, peer[0] * 4 + peer[1]],
                        dst_ref=rs.at[step, me],
                        send_sem=rs_send.at[step],
                        recv_sem=rs_recv.at[step, my_z],
                        device_id=peer,
                        device_id_type=MESH,
                    ).start()
            if hop == 0:
                mine = rs.at[step, me]
                pltpu.make_async_copy(mom.at[step, me], mine, rs_recv.at[step, my_z]).start()

    def solve(step):
        total = jnp.zeros((3, LANES), F32)
        for hop in (2, 1, 3, 0):
            d0 = pl.multiple_of(zs[hop] * PER, PER)
            here = rs.at[step, pl.ds(d0, PER)]
            pltpu.make_async_copy(here, here, rs_recv.at[step, zs[hop]]).wait()
            parts = [rs[step, pl.ds(d0 + 8 * i, 8)].sum(axis=0) for i in range(4)]
            total = total + ((parts[0] + parts[1]) + (parts[2] + parts[3]))
        lane = iota((1, LANES), 1)
        top, middle, bottom = total[0:1], total[1:2], total[2:3]
        second = pltpu.roll(jnp.where(lane < PACK, middle, top), LANES - PACK, axis=1)
        third = pltpu.roll(middle, PACK, axis=1)
        sub = iota((MINE, LANES), 0)
        total = jnp.where(
            sub < 2, jnp.where(sub == 0, top, second), jnp.where(sub == 2, third, bottom)
        )
        high = total.astype(BF16).astype(F32)
        both = jnp.concatenate([high, total - high], axis=0)
        lhs = jnp.concatenate([both, both], axis=1).astype(BF16)
        both = jnp.dot(lhs, link[...], preferred_element_type=F32)
        both = both[0:MINE] + both[MINE : 2 * MINE]
        lane = iota((MINE, LANES), 1)
        group, within = lane // SLOT, lane % SLOT
        system = []
        for v in range(6):
            block = both[:, v * LANES : (v + 1) * LANES]
            system.append(jnp.where(within == 4 * v + group, block + 1.0, block))
        for v in range(6):
            width_of = min(4, 2 * K - 4 * v)
            mine = range(width_of)
            ahead = [pick(system[v], within + SLOT * g) for g in mine]
            pivot = [
                [pick(system[v], jnp.full_like(lane, SLOT * g + 4 * v + b)) for b in mine] for g in mine
            ]
            cols = [[pick(x, group * SLOT + 4 * v + b) for b in mine] for x in system]
            for g in mine:
                unit = 1.0 / pivot[g][g]
                ahead[g] = ahead[g] * unit
                for b in range(g + 1, width_of):
                    pivot[g][b] = pivot[g][b] * unit
                for c in mine:
                    if c != g:
                        ahead[c] = ahead[c] - pivot[c][g] * ahead[g]
                        for b in range(g + 1, width_of):
                            pivot[c][b] = pivot[c][b] - pivot[c][g] * pivot[g][b]
            for u in range(6):
                taken = cols[u][0] * ahead[0]
                for b in range(1, width_of):
                    taken = taken + cols[u][b] * ahead[b]
                system[u] = system[u] - taken
                if u == v:
                    for g in mine:
                        system[u] = jnp.where(group == g, ahead[g], system[u])
        found = jnp.zeros((MINE, LANES), F32)
        for v in range(6):
            got = pick(system[v], (within % 4) * SLOT + 2 * K)
            found = jnp.where((within // 4 == v) & (within < 2 * K), got, found)
        found = jnp.where(iota((MINE, LANES), 0) == group, found, 0.0)
        row[step + 1] = row[step] + found.sum(axis=0, keepdims=True)

    @pl.loop(0, ITERS)
    def _(step):
        early, late = (2, 1), (3, 0)
        profiles(step, early, 0)
        profiles(step, late, 1)
        column_sums(early, 0)
        moments = moments_of(0)
        column_sums(late, 1)
        send(step, early, moments)
        send(step, late, moments_of(1))
        solve(step)
        tell_everyone(step + 1)
        sent = mom.at[step, pl.ds(0, NDEV - 1)]
        pltpu.make_async_copy(sent, sent, rs_send.at[step]).wait()
        told = ag.at[step, pl.ds(0, NDEV - 1)]
        pltpu.make_async_copy(told, told, ag_send.at[step]).wait()

    for z in range(PLANES):
        here = ag.at[ITERS, pl.ds(z * PER, PER)]
        pltpu.make_async_copy(here, here, ag_recv.at[ITERS, z]).wait()
    out[...] = ag[ITERS, :, 0, :]
    told = ag.at[ITERS, pl.ds(0, NDEV - 1)]
    pltpu.make_async_copy(told, told, ag_send.at[ITERS]).wait()


def fit(starts, bundle_width, fiber_bundle, amplitude, trace, width, frames, nrow):
    lamps, rows, cols = frames.shape
    vmem = pl.BlockSpec(memory_space=pltpu.VMEM)
    hbm = pl.BlockSpec(memory_space=pltpu.HBM)
    dma = pltpu.SemaphoreType.DMA
    like = lambda space, x: space(x.shape, x.dtype)
    kernel = functools.partial(fit_kernel, lamps, starts.shape[1], bundle_width.shape[0], nrow)
    shape = jax.ShapeDtypeStruct
    return pl.pallas_call(
        kernel,
        out_shape=(
            shape((NDEV, LANES), F32),
            shape((8, cols), F32),
            shape((lamps, LANES, LANES), F32),
            shape((8, LANES), jnp.int32),
            shape((2 * LANES, LANES), BF16),
        ),
        in_specs=[hbm] * 8,
        out_specs=(vmem,) * 5,
        scratch_shapes=[
            like(pltpu.SMEM, starts),
            like(pltpu.SMEM, bundle_width),
            like(pltpu.VMEM, fiber_bundle),
            like(pltpu.VMEM, amplitude),
            like(pltpu.VMEM, trace),
            like(pltpu.VMEM, width),
            pltpu.VMEM((lamps, rows, cols), BF16),
            pltpu.VMEM((cols, LANES), F32),
            pltpu.VMEM((32, NDEV, LANES), F32),
            pltpu.VMEM((MINE, NDEV, LANES), F32),
            pltpu.VMEM((MINE, NDEV, LANES), F32),
            pltpu.VMEM((MINE * NDEV, LANES), F32),
            pltpu.VMEM((2 * LANES, 8 * LANES), BF16),
            pltpu.VMEM((10 * LANES, 2 * LANES), BF16),
            pltpu.VMEM((2, 2 * PER, 8 * LANES), F32),
            pltpu.VMEM((2, 2 * LANES, 10 * LANES), BF16),
            pltpu.VMEM((2 * LANES, 24 * SLOT), BF16),
            pltpu.VMEM((ITERS + 1, 1, LANES), F32),
            pltpu.VMEM((ITERS + 1, NDEV, 1, LANES), F32),
            pltpu.VMEM((ITERS, NDEV, 3, LANES), F32),
            pltpu.VMEM((ITERS, NDEV, 3, LANES), F32),
            dma((lamps,)),
            dma((6,)),
            dma,
            dma((ITERS + 1,)),
            dma((ITERS + 1, PLANES)),
            dma((ITERS,)),
            dma((ITERS, PLANES)),
        ],
        compiler_params=pltpu.CompilerParams(
            collective_id=0, has_side_effects=True, vmem_limit_bytes=24 << 20
        ),
        name="fit",
    )(
        *(
            pltpu.with_memory_space_constraint(x, pltpu.HBM)
            for x in (starts, bundle_width, fiber_bundle, amplitude, trace, width, link_table(), frames)
        )
    )


BLOCK = 16


def residual_kernel(
    lamps,
    flags, coef, rates, litc, ptab, frames,
    trace_out, width_out, out,
    table, xq, shape, done, sem,
):
    me = lax.axis_index("rows") * 4 + lax.axis_index("fib")
    blocks = frames.shape[1] // BLOCK
    cols = frames.shape[2]

    def at(b):
        return pl.ds(pl.multiple_of(b * BLOCK, BLOCK), BLOCK)

    @pl.loop(0, blocks)
    def _(b):
        for lamp in range(lamps):

            @pl.when(flags[lamp, b] == 0)
            def _():
                pltpu.make_async_copy(frames.at[lamp, at(b)], out.at[lamp, at(b)], sem).start()

    mine = coef[pl.ds(me, 1), :]
    for j in range(MINE):
        trace_out[j : j + 1, :] = mine[:, SLOT * j : SLOT * j + K]
        width_out[j : j + 1, :] = mine[:, SLOT * j + K : SLOT * j + 2 * K]

    turned = jnp.transpose(coef[...])
    lane = iota((SLOT, LANES), 1)
    table[3 * SLOT : 4 * SLOT, :] = jnp.zeros((SLOT, cols), BF16)
    for fb in range(4):
        pick = 32 * fb + lane // MINE
        named = jnp.zeros((SLOT, LANES), F32)
        for j in range(MINE):
            got = jnp.take_along_axis(turned[SLOT * j : SLOT * (j + 1), :], pick, axis=1)
            named = jnp.where(lane % MINE == j, got, named)
        for b in range(8):
            here = pl.ds((8 * fb + b) * LANES, LANES)
            got = jnp.take_along_axis(named, lane // PIX + 16 * b, axis=1)
            high, low = split(got)
            table[0:SLOT, here] = high
            table[SLOT : 2 * SLOT, here] = low
            table[2 * SLOT : 3 * SLOT, here] = high
        here = slice(8 * fb * LANES, 8 * (fb + 1) * LANES)
        xq[:, here] = jnp.dot(ptab[...], table[:, here], preferred_element_type=F32)
    offset = (iota((1, LANES), 1) % PIX).astype(F32) - (PIX - 1) / 2.0

    @pl.loop(0, blocks)
    def _(b):
        lit = flags[0, b]
        for lamp in range(1, lamps):
            lit = lit + flags[lamp, b]

        @pl.when(lit > 0)
        def _():
            for i in range(cols // LANES):
                here = slice(i * LANES, (i + 1) * LANES)
                x = xq[at(b), here]
                q = xq[pl.ds(pl.multiple_of(LANES + b * BLOCK, BLOCK), BLOCK), here]
                u = (offset - x) * (jnp.exp(q) * rates[lamps : lamps + 1, here])
                shape[:, here] = jnp.exp(-(u * u))
            for lamp in range(lamps):

                @pl.when(flags[lamp, b] > 0)
                def _():
                    column = litc[lamp, at(b), :]
                    for i in range(cols // LANES):
                        here = slice(i * LANES, (i + 1) * LANES)
                        model = (column * rates[lamp : lamp + 1, here]) * shape[:, here]
                        seen = frames[lamp, at(b), here].astype(F32)
                        done[lamp, at(b), here] = (seen - model).astype(BF16)
                    pltpu.make_async_copy(done.at[lamp, at(b)], out.at[lamp, at(b)], sem).start()

    pltpu.make_async_copy(frames, out, sem).wait()


def residual(flags, coef, rates, litc, ptab, frames):
    lamps, rows, cols = frames.shape
    vmem = pl.BlockSpec(memory_space=pltpu.VMEM)
    smem = pl.BlockSpec(memory_space=pltpu.SMEM)
    hbm = pl.BlockSpec(memory_space=pltpu.HBM)
    small = jax.ShapeDtypeStruct((MINE, K), F32)
    return pl.pallas_call(
        functools.partial(residual_kernel, lamps),
        out_shape=(small, small, jax.ShapeDtypeStruct(frames.shape, BF16)),
        in_specs=[smem, vmem, vmem, vmem, vmem, vmem],
        out_specs=(vmem, vmem, hbm),
        scratch_shapes=[
            pltpu.VMEM((LANES, cols), BF16),
            pltpu.VMEM((2 * LANES, cols), F32),
            pltpu.VMEM((BLOCK, cols), F32),
            pltpu.VMEM((lamps, rows, cols), BF16),
            pltpu.SemaphoreType.DMA,
        ],
        compiler_params=pltpu.CompilerParams(vmem_limit_bytes=24 << 20),
        name="residual",
    )(flags, coef, rates, litc, ptab, frames)


def body(frames, amplitude, line_start, bundle_width, fiber_bundle, trace_coef, width_coef):
    nrow = frames.shape[1] * lax.axis_size("rows")
    bundle = fiber_bundle.reshape(1, -1)
    coef, rates, litc, flags, ptab = fit(
        line_start, bundle_width, bundle, amplitude, trace_coef, width_coef, frames, nrow
    )
    return residual(flags, coef, rates, litc, ptab, frames)


def solution(mesh):
    placed = (
        P("fib", "rows", None),
        P("fib", None),
        P("fib", None),
        P(),
        P(),
        P(("rows", "fib"), None),
        P(("rows", "fib"), None),
    )
    return jax.shard_map(
        body,
        mesh=mesh,
        in_specs=placed,
        out_specs=(P(("rows", "fib"), None), P(("rows", "fib"), None), P("fib", "rows", None)),
        check_vma=False,
    )
```
